512 devices in a mesh: depth: 32 (over z, x), rows: 16 (over y, core).
Axes of the slice: x: 4, y: 8, z: 8, core: 2. Of those that a mesh axis runs over, the one named last changes fastest.
Arguments:
- spectrum: bfloat16 [2, 4096, 4096], P(None, 'rows'), may hold values from -6 to 6
- plane_index: int32 [32], P('depth'), may hold values from 0 to 2047
- kernel_width: int32 [32], P('depth'), may hold values from 1 to 3
- focus_gain: float32 [32], P('depth'), may hold values from 0.5 to 30
Outputs:
- depth_map: float32 [256, 4096], P('rows', 'depth')
- focused: float32 [2, 256, 4096], P(None, 'rows', 'depth')
The draws below stay inside these ranges and needn't reach their ends.
All inputs are finite; a program needn't handle non-finite values.
Results may differ from the reference program's by a relative error of at most 0.0003.
Values may be sent and summed in bfloat16 or wider, within the bound.
No kernel may reach another device: no remote copies, remote signals or barrier semaphores. Data moves between devices by JAX's collectives and lax.ppermute only.
A program may use at most 192 MiB of HBM per device.

```python
import math
import jax
import jax.numpy as jnp
from jax import lax

NX = 4096
Y_WIN = 256
DEPTHS = 2048
MAXWIDTH = 3
N_PLANES = 32


def draw_focus_gain(key, part):
    values = jnp.exp(jax.random.uniform(key, (N_PLANES,), jnp.float32, jnp.log(0.5), jnp.log(4.0)))
    return values


def place_ends(result, stream_key, smallest, top_value):
    shape = result.shape
    spot = [jax.random.randint(jax.random.fold_in(stream_key, axis), (), 0, shape[axis]) for axis in range(len(shape))]
    result = result.at[tuple(spot)].set(smallest)
    longest = shape.index(max(shape))
    spot[longest] = (spot[longest] + 1) % shape[longest]
    return result.at[tuple(spot)].set(top_value)


def shard_levels(stream_key, shape, pieces, least, top_value):
    def one(dim, shards_of):
        heights = jax.random.uniform(jax.random.fold_in(jax.random.fold_in(stream_key, 6), dim), (shards_of,), jnp.float32, least / len(pieces), top_value / len(pieces))
        return jnp.repeat(jnp.exp(heights), shape[dim] // shards_of).reshape((-1,) + (1,) * (len(shape) - dim - 1))

    factor_of = one(*pieces[0])
    for cut in pieces[1:]:
        factor_of = factor_of * one(*cut)
    return factor_of


def centred(rng, dims, spread, bound, split=(), kind=jnp.bfloat16):
    level = shard_levels(rng, dims, split, -0.22, 0.18) if split else 1.0
    result = jax.random.normal(rng, dims, jnp.float32) * spread * level
    return jnp.minimum(jnp.maximum(result, -bound), bound).astype(kind)


def setup_inputs(seed: int = 0) -> dict:
    keys = jax.random.split(jax.random.key(seed), 5)
    return {
        "spectrum": centred(keys[0], (2, NX, NX), 1.0, 6.0, ((1, 16),)),
        "plane_index": place_ends(jax.random.randint(keys[1], (N_PLANES,), 0, DEPTHS), jax.random.fold_in(keys[1], 1), 0, DEPTHS - 1).astype(jnp.int32),
        "kernel_width": place_ends(jax.random.randint(keys[2], (N_PLANES,), 1, MAXWIDTH + 1), jax.random.fold_in(keys[2], 1), 1, MAXWIDTH).astype(jnp.int32),
        "focus_gain": draw_focus_gain(jax.random.fold_in(keys[4], 71), 0),
    }


def line_phase(plane_index, freqs):
    signed = jnp.where(freqs < NX // 2, freqs, freqs - NX)
    square = signed * signed
    upper_part = (square // NX)[None, :]
    lower_part = (square % NX)[None, :]
    depth_col = plane_index[:, None]
    turns = (depth_col * lower_part + NX * ((depth_col * upper_part) % NX)) % (NX * NX)
    return turns.astype(jnp.float32) * (-2.0 * math.pi / (NX * NX))


def sobel_energy(padded):
    vertical = padded[..., :-2, :] + 2.0 * padded[..., 1:-1, :] + padded[..., 2:, :]
    across = vertical[..., :, 2:] - vertical[..., :, :-2]
    horizontal = padded[..., :, :-2] + 2.0 * padded[..., :, 1:-1] + padded[..., :, 2:]
    downward = horizontal[..., 2:, :] - horizontal[..., :-2, :]
    return across * across + downward * downward


def smooth_columns(energy, radius):
    extent = energy.shape[-1]
    padded = jnp.pad(energy, [(0, 0)] * (energy.ndim - 1) + [(MAXWIDTH, MAXWIDTH)])
    summed = jnp.zeros_like(energy)
    for offset in range(-MAXWIDTH, MAXWIDTH + 1):
        inside = (abs(offset) <= radius).astype(jnp.float32)
        summed = summed + inside * padded[..., MAXWIDTH + offset:MAXWIDTH + offset + extent]
    return summed / (2 * radius + 1).astype(jnp.float32)


def reference(spectrum, plane_index, kernel_width, focus_gain):
    spectra = spectrum.astype(jnp.float32)
    freqs = jnp.arange(NX, dtype=jnp.int32)

    def advance(records, inputs):
        depth_number, radius, sharpness = inputs
        phases = line_phase(depth_number[None], freqs)[0]
        cosine = jnp.cos(phases)
        sine_part = jnp.sin(phases)
        factor_real = cosine[:, None] * cosine[None, :] - sine_part[:, None] * sine_part[None, :]
        factor_imag = cosine[:, None] * sine_part[None, :] + sine_part[:, None] * cosine[None, :]
        rot_real = spectra[0] * factor_real - spectra[1] * factor_imag
        rot_imag = spectra[0] * factor_imag + spectra[1] * factor_real
        picture = jnp.fft.ifft2(lax.complex(rot_real, rot_imag))[:Y_WIN] * NX
        real_part = jnp.real(picture)
        imag_part = jnp.imag(picture)
        intensity = real_part * real_part + imag_part * imag_part
        energy = sobel_energy(jnp.pad(intensity, 1))
        scores = sharpness * jnp.log(1.0 + smooth_columns(energy, radius))
        highest, summed, depth_sum, real_sum, imag_sum = records
        peak = jnp.maximum(highest, scores)
        former = jnp.exp(highest - peak)
        latest = jnp.exp(scores - peak)
        depth_value = depth_number.astype(jnp.float32) / DEPTHS
        updated = (peak, summed * former + latest, depth_sum * former + latest * depth_value,
                   real_sum * former + latest * real_part, imag_sum * former + latest * imag_part)
        return updated, None

    starting = jnp.full((Y_WIN, NX), -1e30, jnp.float32)
    zeros_grid = jnp.zeros((Y_WIN, NX), jnp.float32)
    records, unused = lax.scan(advance, (starting, zeros_grid, zeros_grid, zeros_grid, zeros_grid),
                               (plane_index, kernel_width, focus_gain))
    highest, summed, depth_sum, real_sum, imag_sum = records
    depth_map = depth_sum / summed
    focused = jnp.stack([real_sum / summed, imag_sum / summed])
    return depth_map, focused
```

```python
import math

import jax
import jax.numpy as jnp
from jax import lax
from jax.experimental import pallas as pl
from jax.experimental.pallas import tpu as pltpu
from jax.sharding import PartitionSpec as P

NX = 4096
Y_WIN = 256
DEPTHS = 2048
MAXWIDTH = 3
TURN = NX * NX
HALF = 256
BLOCKS = 8
F32 = jnp.float32
BF16 = jnp.bfloat16
VMEM_LIMIT = 60 * 1024 * 1024


def cos_sin(turns):
    quarter = (turns + (1 << 21)) >> 22
    rest = turns - (quarter << 22)
    x = rest.astype(F32) * (2.0 * math.pi / TURN)
    x2 = x * x
    s = x * (1.0 + x2 * (-1.0 / 6 + x2 * (1.0 / 120 + x2 * (-1.0 / 5040 + x2 * (1.0 / 362880)))))
    c = 1.0 + x2 * (-0.5 + x2 * (1.0 / 24 + x2 * (-1.0 / 720 + x2 * (1.0 / 40320 - x2 * (1.0 / 3628800)))))
    odd = (quarter & 1) == 1
    cos_v = jnp.where(odd, s, c)
    sin_v = jnp.where(odd, c, s)
    cos_v = jnp.where(((quarter + 1) & 2) == 2, -cos_v, cos_v)
    sin_v = jnp.where((quarter & 2) == 2, -sin_v, sin_v)
    return cos_v, sin_v


def chirp_turns(z, s):
    square = s * s
    return (z * (square & (NX - 1)) + NX * ((z * (square >> 12)) & (NX - 1))) & (TURN - 1)


def pieces(value):
    high = value.astype(BF16)
    rest = value - high.astype(F32)
    mid = rest.astype(BF16)
    low = (rest - mid.astype(F32)).astype(BF16)
    return high, mid, low


def dot(a, b):
    return jnp.dot(a, b, preferred_element_type=F32)


def six(left, right):
    return (
        (dot(left[0], right[2]) + dot(left[2], right[0]) + dot(left[1], right[1]))
        + (dot(left[0], right[1]) + dot(left[1], right[0]))
        + dot(left[0], right[0])
    )


def pick_kernel(place_ref, spec_ref, out_ref):
    row_place = place_ref[1]
    q = lax.broadcasted_iota(jnp.int32, (128, 128), 0)
    lane = lax.broadcasted_iota(jnp.int32, (128, 128), 1)
    sort = (lane == (q >> 3) + 16 * (q & 7)).astype(F32).astype(BF16)
    i = lax.broadcasted_iota(jnp.int32, (HALF, HALF), 0)
    l = lax.broadcasted_iota(jnp.int32, (HALF, HALF), 1)
    source = jnp.where(row_place < BLOCKS, l, (HALF - l) & (HALF - 1))
    turn = (i == source).astype(F32).astype(BF16)
    both = []
    for c in range(2):
        picked = lax.dot_general(
            sort, spec_ref[c], (((1,), (1,)), ((), ())), preferred_element_type=F32
        )
        both.append(dot(picked.astype(BF16), turn).reshape(16, 8, HALF))
    out_ref[...] = jnp.concatenate(both, axis=1).astype(BF16)


def table_kernel(tab_ref, row_ref, twist_ref, base_c, base_s):
    b = pl.program_id(0)
    l = lax.broadcasted_iota(jnp.int32, (HALF, HALF), 0)
    y = lax.broadcasted_iota(jnp.int32, (HALF, HALF), 1)

    @pl.when(b == 0)
    def _():
        c, s = cos_sin((l * y & (NX - 1)) << 12)
        base_c[...] = c
        base_s[...] = s
        c, s = cos_sin((l * y & 255) << 16)
        for n, part in enumerate(pieces(c)):
            row_ref[0, n] = part
        for n, part in enumerate(pieces(s)):
            row_ref[1, n] = part
        r = lax.broadcasted_iota(jnp.int32, (16, HALF), 0)
        x = lax.broadcasted_iota(jnp.int32, (16, HALF), 1)
        c, s = cos_sin((r * x & (NX - 1)) << 12)
        twist_ref[0] = c * (1.0 / NX)
        twist_ref[1] = s * (1.0 / NX)

    lane = lax.broadcasted_iota(jnp.int32, (8, HALF), 1)
    c16, s16 = cos_sin((b * lane & 15) << 20)
    c16, s16 = c16[0:1], s16[0:1]
    cosine = base_c[...] * c16 - base_s[...] * s16
    sine = base_s[...] * c16 + base_c[...] * s16
    nyquist = (1 - 2 * (y & 1)).astype(F32)
    sine = jnp.where((l == 0) & (b == 0), nyquist, sine)
    for n, part in enumerate(pieces(cosine)):
        tab_ref[0, 0, n] = part
    for n, part in enumerate(pieces(sine)):
        tab_ref[0, 1, n] = part


def column_kernel(spec_ref, z_ref, tab_ref, out_ref, acc):
    b = pl.program_id(0)
    lane = lax.broadcasted_iota(jnp.int32, (32, HALF), 1)
    special = (lane == 0) & (b == 0)
    z = jnp.concatenate([z_ref[:, 0, :], z_ref[:, 0, :]], axis=1)
    s = jnp.where(special, NX // 2, b * HALF + lane)
    c_o, s_o = cos_sin(chirp_turns(z, s))
    s_o = -s_o
    c_e = jnp.where(special, 1.0, c_o)
    s_e = jnp.where(special, 0.0, s_o)

    lane16 = lax.broadcasted_iota(jnp.int32, (16, HALF), 1)
    plus = spec_ref[b].astype(F32)
    last = spec_ref[15 - b].astype(F32)
    first = spec_ref[jnp.where(b == 0, 8, 16 - b)].astype(F32)
    minus = jnp.where(lane16 == 0, first, last)
    corner = (lane16 == 0) & (b == 0)
    even = jnp.where(corner, plus, plus + minus)
    odd = plus - minus
    o_re = jnp.where(corner[:8], minus[:8], -odd[8:])
    o_im = jnp.where(corner[:8], minus[8:], odd[:8])
    e_re, e_im = even[:8], even[8:]

    def turned(re, im, c, s):
        c, s = c[:, None, :], s[:, None, :]
        t_re = (re[None] * c - im[None] * s).reshape(HALF, HALF)
        t_im = (re[None] * s + im[None] * c).reshape(HALF, HALF)
        return t_re, t_im

    parts = []
    for t, (re, im, c, s) in enumerate(((e_re, e_im, c_e, s_e), (o_re, o_im, c_o, s_o))):
        for half, value in enumerate(turned(re, im, c, s)):
            parts.append((half, six(pieces(value), [tab_ref[0, t, n] for n in range(3)])))
    for half in range(2):
        total = parts[half][1] + parts[half + 2][1]

        @pl.when(b == 0)
        def _():
            acc[half] = total

        @pl.when(b > 0)
        def _():
            acc[half] = acc[half] + total

    @pl.when(b == BLOCKS - 1)
    def _():
        for half in range(2):
            out_ref[:, half] = acc[half].reshape(32, 8, HALF)


def band_kernel(place_ref, in_ref, out_ref, re_s, im_s):
    row_place, z = place_ref[0], place_ref[1]
    v = row_place + 16 * lax.broadcasted_iota(jnp.int32, (8, HALF), 1)
    signed = jnp.where(v < NX // 2, v, v - NX)
    c, s = cos_sin(chirp_turns(z, signed))
    c, s = c[0:1], -s[0:1]
    re = in_ref[:, 0].reshape(HALF, HALF).T
    im = in_ref[:, 1].reshape(HALF, HALF).T
    re_s[...] = re * c - im * s
    im_s[...] = re * s + im * c
    zero = jnp.zeros((1, HALF), F32)
    for r in range(16):
        out_ref[r, 0:16] = re_s[16 * r : 16 * r + 16]
        out_ref[r, 16:32] = im_s[16 * r : 16 * r + 16]
        out_ref[r, 32:40] = jnp.zeros((8, HALF), F32)
        out_ref[r, 32:33] = re_s[16 * r - 1 : 16 * r] if r > 0 else zero
        out_ref[r, 33:34] = re_s[16 * r + 16 : 16 * r + 17] if r < 15 else zero
        out_ref[r, 36:37] = im_s[16 * r - 1 : 16 * r] if r > 0 else zero
        out_ref[r, 37:38] = im_s[16 * r + 16 : 16 * r + 17] if r < 15 else zero


def times_i(v):
    return -v[1], v[0]


def add(a, b):
    return a[0] + b[0], a[1] + b[1]


def sub(a, b):
    return a[0] - b[0], a[1] - b[1]


def times(a, c, s):
    return a[0] * c - a[1] * s, a[0] * s + a[1] * c


def four(a0, a1, a2, a3):
    p, q, m, n = add(a0, a2), add(a1, a3), sub(a0, a2), times_i(sub(a1, a3))
    return add(p, q), add(m, n), sub(p, q), sub(m, n)


def sixteen(a):
    inner = [four(a[r], a[r + 4], a[r + 8], a[r + 12]) for r in range(4)]
    out = [None] * 16
    for k in range(4):
        row = []
        for r in range(4):
            t = r * k
            v = inner[r][k]
            row.append(v if t == 0 else times(v, math.cos(math.pi * t / 8), math.sin(math.pi * t / 8)))
        for m, v in enumerate(four(*row)):
            out[k + 4 * m] = v
    return out


def row_kernel(width_ref, gain_ref, in_ref, row_ref, twist_ref, out_ref, a_s, b_s, power):
    left = pieces(in_ref[...].reshape(640, HALF))
    a_s[...] = six(left, [row_ref[0, n] for n in range(3)]).reshape(16, 40, HALF)
    b_s[...] = six(left, [row_ref[1, n] for n in range(3)]).reshape(16, 40, HALF)
    for half in range(2):
        lanes = slice(128 * half, 128 * half + 128)
        for band in range(3):
            values = []
            for r in range(16):
                if band < 2:
                    top, low = slice(8 * band, 8 * band + 8), slice(16 + 8 * band, 24 + 8 * band)
                    re = a_s[r, top, lanes] - b_s[r, low, lanes]
                    im = b_s[r, top, lanes] + a_s[r, low, lanes]
                else:
                    a, b = a_s[r, 32:40, lanes], b_s[r, 32:40, lanes]
                    re = a - pltpu.roll(b, 4, 0)
                    im = b + pltpu.roll(a, 4, 0)
                values.append(times((re, im), twist_ref[0, r : r + 1, lanes], twist_ref[1, r : r + 1, lanes]))
            for k, (re, im) in enumerate(sixteen(values)):
                target = 2 * k + half
                if band < 2:
                    out_ref[target, 1, 8 * band : 8 * band + 8] = re
                    out_ref[target, 2, 8 * band : 8 * band + 8] = im
                power[8 * band : 8 * band + 8, 128 * target : 128 * target + 128] = re * re + im * im
    here = power[0:16]
    row = lax.broadcasted_iota(jnp.int32, (16, NX), 0)
    lane = lax.broadcasted_iota(jnp.int32, (16, NX), 1)
    up = jnp.where(row == 0, power[16:17], pltpu.roll(here, 1, 0))
    down = jnp.where(row == 15, power[17:18], pltpu.roll(here, 15, 0))

    def moved(v, offset):
        if offset > 0:
            return jnp.where(lane < NX - offset, pltpu.roll(v, NX - offset, 1), 0.0)
        return jnp.where(lane >= -offset, pltpu.roll(v, -offset, 1), 0.0)

    vertical = up + 2.0 * here + down
    step = down - up
    across = moved(vertical, 1) - moved(vertical, -1)
    downward = moved(step, -1) + 2.0 * step + moved(step, 1)
    energy = across * across + downward * downward
    radius = width_ref[0]
    total = energy
    for offset in range(1, MAXWIDTH + 1):
        inside = (offset <= radius).astype(F32)
        total = total + inside * (moved(energy, -offset) + moved(energy, offset))
    smoothed = total / (2 * radius + 1).astype(F32)
    scores = gain_ref[0] * jnp.log(1.0 + smoothed)
    for target in range(32):
        out_ref[target, 0] = scores[:, 128 * target : 128 * target + 128]


def merge_kernel(in_ref, z_ref, depth_ref, focus_ref):
    peak = jnp.max(in_ref[:, 0], axis=0)
    weights = [jnp.exp(in_ref[p, 0] - peak) for p in range(32)]
    total = sum(weights[1:], weights[0])
    depth = sum(w * (z_ref[p].astype(F32) * (1.0 / DEPTHS)) for p, w in enumerate(weights))
    depth_ref[...] = depth / total
    focus_ref[0] = sum(w * in_ref[p, 1] for p, w in enumerate(weights)) / total
    focus_ref[1] = sum(w * in_ref[p, 2] for p, w in enumerate(weights)) / total


def params():
    return pltpu.CompilerParams(vmem_limit_bytes=VMEM_LIMIT)


def whole(shape):
    return pl.BlockSpec(shape, lambda *_: (0,) * len(shape))


def cost(flops, size):
    return pl.CostEstimate(flops=flops, bytes_accessed=size, transcendentals=0)


def shards(spectrum, plane_index, kernel_width, focus_gain):
    depth_place = lax.axis_index("depth")
    row_place = lax.axis_index("rows")
    z_mine = jnp.broadcast_to(plane_index[:, None, None], (32, 1, 128))
    z_all = lax.all_to_all(z_mine, "depth", split_axis=0, concat_axis=0, tiled=True)

    picked = pl.pallas_call(
        pick_kernel,
        grid_spec=pltpu.PrefetchScalarGridSpec(
            num_scalar_prefetch=1,
            grid=(1,),
            in_specs=[pl.BlockSpec((2, HALF, 128), lambda i, place: (0, 0, place[0]))],
            out_specs=whole((16, 16, HALF)),
        ),
        out_shape=jax.ShapeDtypeStruct((16, 16, HALF), BF16),
        compiler_params=params(),
        cost_estimate=cost(50_000_000, 300_000),
        name="pick",
    )(jnp.stack([depth_place, row_place]).astype(jnp.int32), spectrum)
    columns = lax.all_to_all(picked, "rows", split_axis=0, concat_axis=0, tiled=True)

    tables, row_table, twist = pl.pallas_call(
        table_kernel,
        grid=(BLOCKS,),
        in_specs=[],
        out_specs=[
            pl.BlockSpec((1, 2, 3, HALF, HALF), lambda b: (b, 0, 0, 0, 0)),
            whole((2, 3, HALF, HALF)),
            whole((2, 16, HALF)),
        ],
        out_shape=[
            jax.ShapeDtypeStruct((BLOCKS, 2, 3, HALF, HALF), BF16),
            jax.ShapeDtypeStruct((2, 3, HALF, HALF), BF16),
            jax.ShapeDtypeStruct((2, 16, HALF), F32),
        ],
        scratch_shapes=[pltpu.VMEM((HALF, HALF), F32), pltpu.VMEM((HALF, HALF), F32)],
        compiler_params=params(),
        cost_estimate=cost(30_000_000, 7_000_000),
        name="tables",
    )()

    strips = pl.pallas_call(
        column_kernel,
        grid=(BLOCKS,),
        in_specs=[
            whole((16, 16, HALF)),
            whole((32, 1, 128)),
            pl.BlockSpec((1, 2, 3, HALF, HALF), lambda b: (b, 0, 0, 0, 0)),
        ],
        out_specs=whole((32, 2, 8, HALF)),
        out_shape=jax.ShapeDtypeStruct((32, 2, 8, HALF), F32),
        scratch_shapes=[pltpu.VMEM((2, HALF, HALF), F32)],
        compiler_params=params(),
        cost_estimate=cost(6_500_000_000, 8_000_000),
        name="columns",
    )(columns, z_all, tables)
    by_plane = lax.all_to_all(strips, "depth", split_axis=0, concat_axis=0, tiled=True)

    bands = pl.pallas_call(
        band_kernel,
        grid_spec=pltpu.PrefetchScalarGridSpec(
            num_scalar_prefetch=1,
            grid=(1,),
            in_specs=[whole((32, 2, 8, HALF))],
            out_specs=whole((16, 40, HALF)),
            scratch_shapes=[pltpu.VMEM((HALF, HALF), F32), pltpu.VMEM((HALF, HALF), F32)],
        ),
        out_shape=jax.ShapeDtypeStruct((16, 40, HALF), F32),
        compiler_params=params(),
        cost_estimate=cost(1_000_000, 1_200_000),
        name="bands",
    )(jnp.stack([row_place.astype(jnp.int32), plane_index[0]]), by_plane)
    rows_in = lax.all_to_all(bands, "rows", split_axis=0, concat_axis=0, tiled=True)

    smem = pl.BlockSpec(memory_space=pltpu.SMEM)
    records = pl.pallas_call(
        row_kernel,
        in_specs=[
            smem,
            smem,
            whole((16, 40, HALF)),
            whole((2, 3, HALF, HALF)),
            whole((2, 16, HALF)),
        ],
        out_specs=whole((32, 3, 16, 128)),
        out_shape=jax.ShapeDtypeStruct((32, 3, 16, 128), F32),
        scratch_shapes=[
            pltpu.VMEM((16, 40, HALF), F32),
            pltpu.VMEM((16, 40, HALF), F32),
            pltpu.VMEM((24, NX), F32),
        ],
        compiler_params=params(),
        cost_estimate=cost(1_000_000_000, 2_200_000),
        name="rows",
    )(kernel_width, focus_gain, rows_in, row_table, twist)
    merged = lax.all_to_all(records, "depth", split_axis=0, concat_axis=0, tiled=True)

    depth_map, focused = pl.pallas_call(
        merge_kernel,
        in_specs=[whole((32, 3, 16, 128)), whole((32, 1, 128))],
        out_specs=[whole((16, 128)), whole((2, 16, 128))],
        out_shape=[
            jax.ShapeDtypeStruct((16, 128), F32),
            jax.ShapeDtypeStruct((2, 16, 128), F32),
        ],
        compiler_params=params(),
        cost_estimate=cost(1_000_000, 900_000),
        name="merge",
    )(merged, z_all)
    return depth_map, focused


def solution(mesh):
    return jax.shard_map(
        shards,
        mesh=mesh,
        in_specs=(P(None, "rows", None), P("depth"), P("depth"), P("depth")),
        out_specs=(P("rows", "depth"), P(None, "rows", "depth")),
        check_vma=False,
    )
```

```python
import math

import jax
import jax.numpy as jnp
from jax import lax
from jax.experimental import pallas as pl
from jax.experimental.pallas import tpu as pltpu
from jax.sharding import PartitionSpec as P

NX = 4096
Y_WIN = 256
DEPTHS = 2048
MAXWIDTH = 3
TURN = NX * NX
HALF = 256
BLOCKS = 8
F32 = jnp.float32
BF16 = jnp.bfloat16
PIECES = 2
ALL = ("depth", "rows")


def cos_sin(turns):
    quarter = (turns + (1 << 21)) >> 22
    rest = turns - (quarter << 22)
    x = rest.astype(F32) * (2.0 * math.pi / TURN)
    x2 = x * x
    s = x * (1.0 + x2 * (-1.0 / 6 + x2 * (1.0 / 120 + x2 * (-1.0 / 5040 + x2 * (1.0 / 362880)))))
    c = 1.0 + x2 * (-0.5 + x2 * (1.0 / 24 + x2 * (-1.0 / 720 + x2 * (1.0 / 40320 - x2 * (1.0 / 3628800)))))
    odd = (quarter & 1) == 1
    cos_v = jnp.where(odd, s, c)
    sin_v = jnp.where(odd, c, s)
    cos_v = jnp.where(((quarter + 1) & 2) == 2, -cos_v, cos_v)
    sin_v = jnp.where((quarter & 2) == 2, -sin_v, sin_v)
    return cos_v, sin_v


def chirp_turns(z, s):
    square = s * s
    return (z * (square & (NX - 1)) + NX * ((z * (square >> 12)) & (NX - 1))) & (TURN - 1)


def pieces(value):
    out = []
    for n in range(PIECES):
        out.append(value.astype(BF16))
        if n < PIECES - 1:
            value = value - out[-1].astype(F32)
    return out


def dot(a, b):
    return jnp.dot(a, b, preferred_element_type=F32)


def product(left, right):
    if PIECES == 2:
        return (dot(left[0], right[1]) + dot(left[1], right[0])) + dot(left[0], right[0])
    return (
        (dot(left[0], right[2]) + dot(left[2], right[0]) + dot(left[1], right[1]))
        + (dot(left[0], right[1]) + dot(left[1], right[0]))
        + dot(left[0], right[0])
    )


def places():
    d, r = lax.axis_index("depth"), lax.axis_index("rows")
    return d, r, (r - d) & 15


def swapped(parts, group):
    count = len(parts)
    lane = lax.broadcasted_iota(jnp.int32, parts[0].shape, 1)
    parts = list(parts)
    step = 1
    while step < count:
        low = ((lane // group) & step) == 0
        for i in range(count):
            if i & step == 0:
                x, y = parts[i], parts[i + step]
                parts[i] = jnp.where(low, x, pltpu.roll(y, group * step, 1))
                parts[i + step] = jnp.where(low, pltpu.roll(x, 128 - group * step, 1), y)
        step *= 2
    return parts


def pick_kernel(z_ref, width_ref, gain_ref, spec_ref, out_ref, buf, sem):
    d, r, j = places()
    copy = pltpu.make_async_copy(
        spec_ref.at[:, pl.ds(pl.multiple_of(128 * (d >> 4), 128), 128), pl.ds(pl.multiple_of(256 * j, 256), 256)],
        buf,
        sem,
    )
    copy.start()
    q = lax.broadcasted_iota(jnp.int32, (256, 256), 0)
    lane = lax.broadcasted_iota(jnp.int32, (256, 256), 1)
    target = q >> 3
    sort = (lane == (target & 15) + 128 * (target >> 4) + 16 * (q & 7)).astype(F32).astype(BF16)
    i = lax.broadcasted_iota(jnp.int32, (128, 128), 0)
    l = lax.broadcasted_iota(jnp.int32, (128, 128), 1)
    source = jnp.where(r < BLOCKS, l, (128 - l) & 127)
    turn = (i == source).astype(F32).astype(BF16)
    row = lax.broadcasted_iota(jnp.int32, (8, 128), 0)
    gain = jnp.full((8, 128), gain_ref[0], F32)
    high = gain.astype(BF16).astype(F32)
    mid = (gain - high).astype(BF16).astype(F32)
    z = z_ref[0]
    extra = jnp.zeros((8, 128), F32)
    values = ((z & ~31).astype(F32), (z & 31).astype(F32), width_ref[0].astype(F32), high, mid, gain - high - mid)
    for n, value in enumerate(values):
        extra = jnp.where(row == n, value, extra)
    copy.wait()
    both = []
    for c in range(2):
        picked = lax.dot_general(sort, buf[c], (((1,), (1,)), ((), ())), preferred_element_type=F32)
        both.append(dot(picked.astype(BF16), turn).reshape(32, 8, 128))
    both.append(jnp.broadcast_to(extra[None], (32, 8, 128)))
    out_ref[...] = jnp.concatenate(both, axis=1).astype(BF16)


def table_kernel(tab_ref, row_ref, twist_ref, base_c, base_s):
    b = pl.program_id(0)
    l = lax.broadcasted_iota(jnp.int32, (HALF, HALF), 0)
    y = lax.broadcasted_iota(jnp.int32, (HALF, HALF), 1)

    @pl.when(b == 0)
    def _():
        c, s = cos_sin((l * y & (NX - 1)) << 12)
        base_c[...] = c
        base_s[...] = s
        number = 16 * (l & 15) + 8 * ((l >> 4) & 1) + 4 * (l >> 7) + ((l >> 5) & 3)
        c, s = cos_sin((number * y & 255) << 16)
        for n, part in enumerate(pieces(c)):
            row_ref[0, n] = part
        for n, part in enumerate(pieces(s)):
            row_ref[1, n] = part
        k = lax.broadcasted_iota(jnp.int32, (16, HALF), 0)
        x = lax.broadcasted_iota(jnp.int32, (16, HALF), 1)
        c, s = cos_sin(((k * x - 256 * k * x) & (NX - 1)) << 12)
        twist_ref[0] = c * (1.0 / NX)
        twist_ref[1] = s * (1.0 / NX)

    lane = lax.broadcasted_iota(jnp.int32, (8, HALF), 1)
    c16, s16 = cos_sin((b * lane & 15) << 20)
    c16, s16 = c16[0:1], s16[0:1]
    cosine = base_c[...] * c16 - base_s[...] * s16
    sine = base_s[...] * c16 + base_c[...] * s16
    nyquist = (1 - 2 * (y & 1)).astype(F32)
    sine = jnp.where((l == 0) & (b == 0), nyquist, sine)
    for n, part in enumerate(pieces(cosine)):
        tab_ref[0, 0, n] = part
    for n, part in enumerate(pieces(sine)):
        tab_ref[0, 1, n] = part


def column_kernel(spec_ref, tab_ref, out_ref, par_ref, acc, par_s, bands):
    b = pl.program_id(0)
    d, r, j = places()

    @pl.when(b == 0)
    def _():
        par_s[...] = spec_ref[:, 16:24].astype(F32).reshape(256, 128)
        rows = [par_s[pl.ds(n, 32, stride=8), :] for n in range(6)]
        par_ref[0] = rows[0] + rows[1]
        par_ref[1] = rows[2]
        par_ref[2] = rows[3] + rows[4] + rows[5]

    lane = lax.broadcasted_iota(jnp.int32, (32, HALF), 1)
    special = (lane == 0) & (b == 0)
    z = par_ref[0].astype(jnp.int32)
    z2 = jnp.concatenate([z, z], axis=1)
    s = jnp.where(special, NX // 2, b * HALF + lane)
    c_o, s_o = cos_sin(chirp_turns(z2, s))
    s_o = -s_o
    c_e = jnp.where(special, 1.0, c_o)
    s_e = jnp.where(special, 0.0, s_o)

    def block(n):
        return spec_ref[(((n >> 1) - j) & 15) + 16 * (n & 1), 0:16].astype(F32)

    lane16 = lax.broadcasted_iota(jnp.int32, (16, HALF), 1)
    plus = jnp.concatenate([block(2 * b), block(2 * b + 1)], axis=1)
    middle = block(31 - 2 * b)
    last = jnp.concatenate([middle, block(30 - 2 * b)], axis=1)
    first = jnp.concatenate([block(jnp.where(b == 0, 16, 32 - 2 * b)), middle], axis=1)
    minus = jnp.where((lane16 & 127) == 0, first, last)
    corner = (lane16 == 0) & (b == 0)
    even = jnp.where(corner, plus, plus + minus)
    odd = plus - minus
    o_re = jnp.where(corner[:8], minus[:8], -odd[8:])
    o_im = jnp.where(corner[:8], minus[8:], odd[:8])
    e_re, e_im = even[:8], even[8:]

    def turned(re, im, c, s):
        re, im = re[:, None, :], im[:, None, :]
        t_re = (re * c[None] - im * s[None]).reshape(HALF, HALF)
        t_im = (re * s[None] + im * c[None]).reshape(HALF, HALF)
        return t_re, t_im

    parts = []
    for t, (re, im, c, s) in enumerate(((e_re, e_im, c_e, s_e), (o_re, o_im, c_o, s_o))):
        for value in turned(re, im, c, s):
            parts.append(product(pieces(value), [tab_ref[0, t, n] for n in range(PIECES)]))
    for half in range(2):
        total = parts[half] + parts[half + 2]

        @pl.when(b == 0)
        def _():
            acc[half] = total

        @pl.when(b > 0)
        def _():
            acc[half] = acc[half] + total

    @pl.when(b == BLOCKS - 1)
    def _():
        lane = lax.broadcasted_iota(jnp.int32, (8, 128), 1)
        group = (lane >> 2) & 3
        plane = z[0:8]
        for n in range(1, 4):
            plane = jnp.where(group == n, z[8 * n : 8 * n + 8], plane)
        v = 256 * j + 128 * (d >> 4) + 16 * (lane >> 4) + (d & 15)
        c, s = cos_sin(chirp_turns(plane, jnp.where(v < NX // 2, v, v - NX)))
        s = -s
        for half in range(2):
            cols = slice(128 * half, 128 * half + 128)
            for part in range(2):
                for n, v in enumerate(swapped([acc[part, 8 * i : 8 * i + 8, cols] for i in range(32)], 4)):
                    bands[part, 32 * half + n] = v
        for n in range(64):
            re, im = bands[0, n], bands[1, n]
            bands[0, n] = re * c - im * s
            bands[1, n] = re * s + im * c
        slot = lane & 3
        for n in range(64):
            zero = jnp.zeros((8, 128), F32)
            above = [bands[part, n - 1] if n > 0 else zero for part in range(2)]
            below = [bands[part, n + 1] if n < 63 else zero for part in range(2)]
            rim = jnp.where(
                slot < 2,
                jnp.where(slot == 0, pltpu.roll(above[0], 125, 1), pltpu.roll(below[0], 1, 1)),
                jnp.where(slot == 2, pltpu.roll(above[1], 127, 1), pltpu.roll(below[1], 3, 1)),
            )
            item = 3 * ((n & 3) * 16 + (n >> 2))
            out_ref[pl.ds(item, 8, stride=192), :] = bands[0, n]
            out_ref[pl.ds(item + 1, 8, stride=192), :] = bands[1, n]
            out_ref[pl.ds(item + 2, 8, stride=192), :] = rim


def times_i(v):
    return -v[1], v[0]


def add(a, b):
    return a[0] + b[0], a[1] + b[1]


def sub(a, b):
    return a[0] - b[0], a[1] - b[1]


def times(a, c, s):
    return a[0] * c - a[1] * s, a[0] * s + a[1] * c


def four(a0, a1, a2, a3):
    p, q, m, n = add(a0, a2), add(a1, a3), sub(a0, a2), times_i(sub(a1, a3))
    return add(p, q), add(m, n), sub(p, q), sub(m, n)


def sixteen(a):
    inner = [four(a[r], a[r + 4], a[r + 8], a[r + 12]) for r in range(4)]
    out = [None] * 16
    for k in range(4):
        row = []
        for r in range(4):
            t = r * k
            v = inner[r][k]
            row.append(v if t == 0 else times(v, math.cos(math.pi * t / 8), math.sin(math.pi * t / 8)))
        for m, v in enumerate(four(*row)):
            out[k + 4 * m] = v
    return out


def row_kernel(in_ref, par_ref, row_ref, twist_ref, out_ref, x_s, a_s, b_s, power, re_s, im_s):
    d, _, _ = places()
    g = d >> 2
    for quad in range(4):
        for piece in range(3):
            rows = []
            for n in range(4):
                for half in range(2):
                    start = 48 * (4 * quad + n + 16 * half) + piece
                    rows.append(in_ref[pl.ds(start, 16, stride=3), :])
            turned = jnp.concatenate(rows, axis=0).T
            for a in range(2):
                parts = swapped([turned[64 * a + 16 * n : 64 * a + 16 * n + 16] for n in range(4)], 32)
                for n, part in enumerate(parts):
                    x_s[4 * quad + n, 16 * piece : 16 * piece + 16, 128 * a : 128 * a + 128] = part
    left = pieces(x_s[...].reshape(768, HALF))
    a_s[...] = product(left, [row_ref[0, n] for n in range(PIECES)]).reshape(16, 48, HALF)
    b_s[...] = product(left, [row_ref[1, n] for n in range(PIECES)]).reshape(16, 48, HALF)
    for half in range(2):
        lanes = slice(128 * half, 128 * half + 128)
        for band in range(4):
            here = slice(8 * band, 8 * band + 8)
            values = []
            for k in range(16):
                if band < 2:
                    low = slice(16 + 8 * band, 24 + 8 * band)
                    re = a_s[k, here, lanes] - b_s[k, low, lanes]
                    im = b_s[k, here, lanes] + a_s[k, low, lanes]
                else:
                    rim = slice(16 + 8 * band, 24 + 8 * band)
                    a, b = a_s[k, rim, lanes], b_s[k, rim, lanes]
                    re = a - pltpu.roll(b, 6, 0)
                    im = b + pltpu.roll(a, 6, 0)
                values.append(times((re, im), twist_ref[0, k : k + 1, lanes], twist_ref[1, k : k + 1, lanes]))
            for k, (re, im) in enumerate(sixteen(values)):
                spot = slice(256 * k + 128 * half, 256 * k + 128 * half + 128)
                if band < 2:
                    re_s[here, spot] = re
                    im_s[here, spot] = im
                power[here, spot] = re * re + im * im
    here = power[0:16]
    rim = power[16:32]
    row = lax.broadcasted_iota(jnp.int32, (16, NX), 0)
    lane = lax.broadcasted_iota(jnp.int32, (16, NX), 1)
    up = jnp.where((row & 3) == 0, rim, pltpu.roll(here, 1, 0))
    down = jnp.where((row & 3) == 3, pltpu.roll(rim, 2, 0), pltpu.roll(here, 15, 0))

    def moved(v, offset):
        if offset > 0:
            return jnp.where(lane < NX - offset, pltpu.roll(v, NX - offset, 1), 0.0)
        return jnp.where(lane >= -offset, pltpu.roll(v, -offset, 1), 0.0)

    row_small = lax.broadcasted_iota(jnp.int32, (16, 128), 0) >> 2

    def of_rows(which):
        value = jnp.zeros((16, 128), F32)
        for n in range(4):
            value = jnp.where(row_small == n, par_ref[which, pl.ds(8 * n + g, 1), :], value)
        return value[:, 0:1]

    depth, radius, gain = of_rows(0) * (1.0 / DEPTHS), of_rows(1), of_rows(2)
    vertical = up + 2.0 * here + down
    step = down - up
    across = moved(vertical, 1) - moved(vertical, -1)
    downward = moved(step, -1) + 2.0 * step + moved(step, 1)
    energy = across * across + downward * downward
    total = energy
    for offset in range(1, MAXWIDTH + 1):
        inside = (offset <= radius).astype(F32)
        total = total + inside * (moved(energy, -offset) + moved(energy, offset))
    smoothed = total / (2.0 * radius + 1.0)
    scores = gain * jnp.log(1.0 + smoothed)
    peak = jnp.maximum(scores[0:8], scores[8:16])
    peak = jnp.maximum(peak, pltpu.roll(peak, 4, 0))
    first, second = jnp.exp(scores[0:8] - peak), jnp.exp(scores[8:16] - peak)

    def joined(v):
        return (v + pltpu.roll(v, 4, 0))[0:4]

    records = (
        peak[0:4],
        joined(first + second),
        joined(first * depth[0:8] + second * depth[8:16]),
        joined(first * re_s[0:8] + second * re_s[8:16]),
        joined(first * im_s[0:8] + second * im_s[8:16]),
    )
    for n, record in enumerate(records):
        for target in range(32):
            out_ref[target, n] = record[:, 128 * target : 128 * target + 128]


def merge_kernel(in_ref, depth_ref, focus_ref):
    for q in range(4):
        spots = [4 * g + q for g in range(8)]
        peak = in_ref[spots[0], 0]
        for n in spots[1:]:
            peak = jnp.maximum(peak, in_ref[n, 0])
        weights = [jnp.exp(in_ref[n, 0] - peak) for n in spots]
        sums = [sum(w * in_ref[n, k] for w, n in zip(weights, spots)) for k in range(1, 5)]
        rows = slice(4 * q, 4 * q + 4)
        depth_ref[rows] = sums[1] / sums[0]
        focus_ref[0, rows] = sums[2] / sums[0]
        focus_ref[1, rows] = sums[3] / sums[0]


def params(mib):
    return pltpu.CompilerParams(vmem_limit_bytes=mib * 1024 * 1024)


def whole(shape):
    return pl.BlockSpec(shape, lambda *_: (0,) * len(shape))


def cost(flops, size):
    return pl.CostEstimate(flops=flops, bytes_accessed=size, transcendentals=0)


def shards(spectrum, plane_index, kernel_width, focus_gain):
    smem = pl.BlockSpec(memory_space=pltpu.SMEM)
    picked = pl.pallas_call(
        pick_kernel,
        in_specs=[smem, smem, smem, pl.BlockSpec(memory_space=pl.ANY)],
        out_specs=whole((32, 24, 128)),
        out_shape=jax.ShapeDtypeStruct((32, 24, 128), BF16),
        scratch_shapes=[pltpu.VMEM((2, 128, 256), BF16), pltpu.SemaphoreType.DMA(())],
        compiler_params=params(58),
        cost_estimate=cost(50_000_000, 300_000),
        name="pick",
    )(plane_index, kernel_width, focus_gain, spectrum)
    groups = [[16 * d + (d + j) % 16 for d in range(32)] for j in range(16)]
    columns = lax.all_to_all(
        picked, ALL, split_axis=0, concat_axis=0, tiled=True, axis_index_groups=groups
    )

    tables, row_table, twist = pl.pallas_call(
        table_kernel,
        grid=(BLOCKS,),
        in_specs=[],
        out_specs=[
            pl.BlockSpec((1, 2, PIECES, HALF, HALF), lambda b: (b, 0, 0, 0, 0)),
            whole((2, PIECES, HALF, HALF)),
            whole((2, 16, HALF)),
        ],
        out_shape=[
            jax.ShapeDtypeStruct((BLOCKS, 2, PIECES, HALF, HALF), BF16),
            jax.ShapeDtypeStruct((2, PIECES, HALF, HALF), BF16),
            jax.ShapeDtypeStruct((2, 16, HALF), F32),
        ],
        scratch_shapes=[pltpu.VMEM((HALF, HALF), F32), pltpu.VMEM((HALF, HALF), F32)],
        compiler_params=params(16),
        cost_estimate=cost(30_000_000, 5_000_000),
        name="tables",
    )()

    messages, planes = pl.pallas_call(
        column_kernel,
        grid=(BLOCKS,),
        in_specs=[
            whole((32, 24, 128)),
            pl.BlockSpec((1, 2, PIECES, HALF, HALF), lambda b: (b, 0, 0, 0, 0)),
        ],
        out_specs=[whole((1536, 128)), whole((3, 32, 128))],
        out_shape=[
            jax.ShapeDtypeStruct((1536, 128), F32),
            jax.ShapeDtypeStruct((3, 32, 128), F32),
        ],
        scratch_shapes=[
            pltpu.VMEM((2, HALF, HALF), F32),
            pltpu.VMEM((256, 128), F32),
            pltpu.VMEM((2, 64, 8, 128), F32),
        ],
        compiler_params=params(50),
        cost_estimate=cost(6_500_000_000, 8_000_000),
        name="columns",
    )(columns, tables)
    arrived = lax.all_to_all(
        messages.reshape(512, 1, 384), ALL, split_axis=0, concat_axis=0, tiled=True
    )

    records = pl.pallas_call(
        row_kernel,
        in_specs=[
            whole((1536, 128)),
            whole((3, 32, 128)),
            whole((2, PIECES, HALF, HALF)),
            whole((2, 16, HALF)),
        ],
        out_specs=whole((32, 5, 4, 128)),
        out_shape=jax.ShapeDtypeStruct((32, 5, 4, 128), F32),
        scratch_shapes=[
            pltpu.VMEM((16, 48, HALF), F32),
            pltpu.VMEM((16, 48, HALF), F32),
            pltpu.VMEM((16, 48, HALF), F32),
            pltpu.VMEM((32, NX), F32),
            pltpu.VMEM((16, NX), F32),
            pltpu.VMEM((16, NX), F32),
        ],
        compiler_params=params(24),
        cost_estimate=cost(1_000_000_000, 2_200_000),
        name="rows",
    )(arrived.reshape(1536, 128), planes, row_table, twist)
    merged = lax.all_to_all(records, "depth", split_axis=0, concat_axis=0, tiled=True)

    depth_map, focused = pl.pallas_call(
        merge_kernel,
        in_specs=[whole((32, 5, 4, 128))],
        out_specs=[whole((16, 128)), whole((2, 16, 128))],
        out_shape=[
            jax.ShapeDtypeStruct((16, 128), F32),
            jax.ShapeDtypeStruct((2, 16, 128), F32),
        ],
        compiler_params=params(4),
        cost_estimate=cost(1_000_000, 500_000),
        name="merge",
    )(merged)
    return depth_map, focused


def solution(mesh):
    return jax.shard_map(
        shards,
        mesh=mesh,
        in_specs=(P(None, "rows", None), P("depth"), P("depth"), P("depth")),
        out_specs=(P("rows", "depth"), P(None, "rows", "depth")),
        check_vma=False,
    )
```

```python
import math

import jax
import jax.numpy as jnp
from jax import lax
from jax.experimental import pallas as pl
from jax.experimental.pallas import tpu as pltpu
from jax.sharding import PartitionSpec as P

NX = 4096
Y_WIN = 256
DEPTHS = 2048
MAXWIDTH = 3
TURN = NX * NX
HALF = 256
BLOCKS = 8
F32 = jnp.float32
BF16 = jnp.bfloat16
PIECES = 2
ALL = ("depth", "rows")


def cos_sin(turns):
    quarter = (turns + (1 << 21)) >> 22
    rest = turns - (quarter << 22)
    x = rest.astype(F32) * (2.0 * math.pi / TURN)
    x2 = x * x
    s = x * (1.0 + x2 * (-1.0 / 6 + x2 * (1.0 / 120 + x2 * (-1.0 / 5040 + x2 * (1.0 / 362880)))))
    c = 1.0 + x2 * (-0.5 + x2 * (1.0 / 24 + x2 * (-1.0 / 720 + x2 * (1.0 / 40320 - x2 * (1.0 / 3628800)))))
    odd = (quarter & 1) == 1
    cos_v = jnp.where(odd, s, c)
    sin_v = jnp.where(odd, c, s)
    cos_v = jnp.where(((quarter + 1) & 2) == 2, -cos_v, cos_v)
    sin_v = jnp.where((quarter & 2) == 2, -sin_v, sin_v)
    return cos_v, sin_v


def chirp_turns(z, s):
    square = s * s
    return (z * (square & (NX - 1)) + NX * ((z * (square >> 12)) & (NX - 1))) & (TURN - 1)


def pieces(value):
    out = []
    for n in range(PIECES):
        out.append(value.astype(BF16))
        if n < PIECES - 1:
            value = value - out[-1].astype(F32)
    return out


def dot(a, b):
    return jnp.dot(a, b, preferred_element_type=F32)


def product(left, right):
    if PIECES == 2:
        return (dot(left[0], right[1]) + dot(left[1], right[0])) + dot(left[0], right[0])
    return (
        (dot(left[0], right[2]) + dot(left[2], right[0]) + dot(left[1], right[1]))
        + (dot(left[0], right[1]) + dot(left[1], right[0]))
        + dot(left[0], right[0])
    )


def places():
    d, r = lax.axis_index("depth"), lax.axis_index("rows")
    return d, r, (r - d) & 15


def swapped(parts, group):
    count = len(parts)
    lane = lax.broadcasted_iota(jnp.int32, parts[0].shape, 1)
    parts = list(parts)
    step = 1
    while step < count:
        low = ((lane // group) & step) == 0
        for i in range(count):
            if i & step == 0:
                x, y = parts[i], parts[i + step]
                parts[i] = jnp.where(low, x, pltpu.roll(y, group * step, 1))
                parts[i + step] = jnp.where(low, pltpu.roll(x, 128 - group * step, 1), y)
        step *= 2
    return parts


def packed(re, im, rim):
    most = jnp.maximum(jnp.maximum(jnp.abs(re), jnp.abs(im)), jnp.abs(rim))
    small = most < 2.0**-40
    lift = jnp.where(small, 2.0**80, 1.0)
    power = jnp.floor(jnp.log2(jnp.maximum(most * lift, 2.0**-46)) + 0.01).astype(jnp.int32) + 1
    scale = jnp.exp2((18 - power).astype(F32)) * lift

    def whole_number(v):
        return jnp.floor(v + 0.5).astype(jnp.int32)

    a, b, c = whole_number(re * scale), whole_number(im * scale), whole_number(rim * scale * 0.5)
    code = power + jnp.where(small, 128 - 80, 128)
    first = (a << 13) | (code << 5) | (c & 31)
    second = (b << 13) | ((c >> 5) & 0x1FFF)
    return first, second


def unpacked(first, second):
    power = ((first >> 5) & 255) - 128
    small = power < -40
    scale = jnp.exp2((jnp.where(small, power + 80, power) - 18).astype(F32))
    scale = scale * jnp.where(small, 2.0**-80, 1.0)
    c = (((second << 19) >> 19) << 5) + (first & 31)
    return (first >> 13).astype(F32) * scale, (second >> 13).astype(F32) * scale, c.astype(F32) * (scale * 2.0)


def pick_kernel(z_ref, width_ref, gain_ref, spec_ref, out_ref, buf, sem):
    d, r, j = places()
    copy = pltpu.make_async_copy(
        spec_ref.at[:, pl.ds(pl.multiple_of(128 * (d >> 4), 128), 128), pl.ds(pl.multiple_of(256 * j, 256), 256)],
        buf,
        sem,
    )
    copy.start()
    q = lax.broadcasted_iota(jnp.int32, (256, 256), 0)
    lane = lax.broadcasted_iota(jnp.int32, (256, 256), 1)
    target = q >> 3
    sort = (lane == (target & 15) + 128 * (target >> 4) + 16 * (q & 7)).astype(F32).astype(BF16)
    i = lax.broadcasted_iota(jnp.int32, (128, 128), 0)
    l = lax.broadcasted_iota(jnp.int32, (128, 128), 1)
    source = jnp.where(r < BLOCKS, l, (128 - l) & 127)
    turn = (i == source).astype(F32).astype(BF16)
    row = lax.broadcasted_iota(jnp.int32, (8, 128), 0)
    gain = jnp.full((8, 128), gain_ref[0], F32)
    high = gain.astype(BF16).astype(F32)
    mid = (gain - high).astype(BF16).astype(F32)
    z = z_ref[0]
    extra = jnp.zeros((8, 128), F32)
    values = ((z & ~31).astype(F32), (z & 31).astype(F32), width_ref[0].astype(F32), high, mid, gain - high - mid)
    for n, value in enumerate(values):
        extra = jnp.where(row == n, value, extra)
    copy.wait()
    both = []
    for c in range(2):
        picked = lax.dot_general(sort, buf[c], (((1,), (1,)), ((), ())), preferred_element_type=F32)
        both.append(dot(picked.astype(BF16), turn).reshape(32, 8, 128))
    both.append(jnp.broadcast_to(extra[None], (32, 8, 128)))
    out_ref[...] = jnp.concatenate(both, axis=1).astype(BF16)


def table_kernel(tab_ref, row_ref, twist_ref, base_c, base_s):
    b = pl.program_id(0)
    l = lax.broadcasted_iota(jnp.int32, (HALF, HALF), 0)
    y = lax.broadcasted_iota(jnp.int32, (HALF, HALF), 1)

    @pl.when(b == 0)
    def _():
        c, s = cos_sin((l * y & (NX - 1)) << 12)
        base_c[...] = c
        base_s[...] = s
        number = 16 * (l & 15) + 8 * ((l >> 4) & 1) + 4 * (l >> 7) + ((l >> 5) & 3)
        c, s = cos_sin((number * y & 255) << 16)
        for n, part in enumerate(pieces(c)):
            row_ref[0, n] = part
        for n, part in enumerate(pieces(s)):
            row_ref[1, n] = part
        k = lax.broadcasted_iota(jnp.int32, (16, HALF), 0)
        x = lax.broadcasted_iota(jnp.int32, (16, HALF), 1)
        c, s = cos_sin(((k * x - 256 * k * x) & (NX - 1)) << 12)
        twist_ref[0] = c * (1.0 / NX)
        twist_ref[1] = s * (1.0 / NX)

    lane = lax.broadcasted_iota(jnp.int32, (8, HALF), 1)
    c16, s16 = cos_sin((b * lane & 15) << 20)
    c16, s16 = c16[0:1], s16[0:1]
    cosine = base_c[...] * c16 - base_s[...] * s16
    sine = base_s[...] * c16 + base_c[...] * s16
    nyquist = (1 - 2 * (y & 1)).astype(F32)
    sine = jnp.where((l == 0) & (b == 0), nyquist, sine)
    for n, part in enumerate(pieces(cosine)):
        tab_ref[0, 0, n] = part
    for n, part in enumerate(pieces(sine)):
        tab_ref[0, 1, n] = part


def column_kernel(spec_ref, tab_ref, out_ref, par_ref, acc, par_s, bands):
    b = pl.program_id(0)
    d, r, j = places()

    @pl.when(b == 0)
    def _():
        par_s[...] = spec_ref[:, 16:24].astype(F32).reshape(256, 128)
        rows = [par_s[pl.ds(n, 32, stride=8), :] for n in range(6)]
        par_ref[0] = rows[0] + rows[1]
        par_ref[1] = rows[2]
        par_ref[2] = rows[3] + rows[4] + rows[5]

    lane = lax.broadcasted_iota(jnp.int32, (32, HALF), 1)
    special = (lane == 0) & (b == 0)
    z = par_ref[0].astype(jnp.int32)
    z2 = jnp.concatenate([z, z], axis=1)
    s = jnp.where(special, NX // 2, b * HALF + lane)
    c_o, s_o = cos_sin(chirp_turns(z2, s))
    s_o = -s_o
    c_e = jnp.where(special, 1.0, c_o)
    s_e = jnp.where(special, 0.0, s_o)

    def block(n):
        return spec_ref[(((n >> 1) - j) & 15) + 16 * (n & 1), 0:16].astype(F32)

    lane16 = lax.broadcasted_iota(jnp.int32, (16, HALF), 1)
    plus = jnp.concatenate([block(2 * b), block(2 * b + 1)], axis=1)
    middle = block(31 - 2 * b)
    last = jnp.concatenate([middle, block(30 - 2 * b)], axis=1)
    first = jnp.concatenate([block(jnp.where(b == 0, 16, 32 - 2 * b)), middle], axis=1)
    minus = jnp.where((lane16 & 127) == 0, first, last)
    corner = (lane16 == 0) & (b == 0)
    even = jnp.where(corner, plus, plus + minus)
    odd = plus - minus
    o_re = jnp.where(corner[:8], minus[:8], -odd[8:])
    o_im = jnp.where(corner[:8], minus[8:], odd[:8])
    e_re, e_im = even[:8], even[8:]

    def turned(re, im, c, s):
        re, im = re[:, None, :], im[:, None, :]
        t_re = (re * c[None] - im * s[None]).reshape(HALF, HALF)
        t_im = (re * s[None] + im * c[None]).reshape(HALF, HALF)
        return t_re, t_im

    parts = []
    for t, (re, im, c, s) in enumerate(((e_re, e_im, c_e, s_e), (o_re, o_im, c_o, s_o))):
        for value in turned(re, im, c, s):
            parts.append(product(pieces(value), [tab_ref[0, t, n] for n in range(PIECES)]))
    for half in range(2):
        total = parts[half] + parts[half + 2]

        @pl.when(b == 0)
        def _():
            acc[half] = total

        @pl.when(b > 0)
        def _():
            acc[half] = acc[half] + total

    @pl.when(b == BLOCKS - 1)
    def _():
        lane = lax.broadcasted_iota(jnp.int32, (8, 128), 1)
        group = (lane >> 2) & 3
        plane = z[0:8]
        for n in range(1, 4):
            plane = jnp.where(group == n, z[8 * n : 8 * n + 8], plane)
        v = 256 * j + 128 * (d >> 4) + 16 * (lane >> 4) + (d & 15)
        c, s = cos_sin(chirp_turns(plane, jnp.where(v < NX // 2, v, v - NX)))
        s = -s
        for half in range(2):
            cols = slice(128 * half, 128 * half + 128)
            for part in range(2):
                for n, v in enumerate(swapped([acc[part, 8 * i : 8 * i + 8, cols] for i in range(32)], 4)):
                    bands[part, 32 * half + n] = v
        for n in range(64):
            re, im = bands[0, n], bands[1, n]
            bands[0, n] = re * c - im * s
            bands[1, n] = re * s + im * c
        slot = lane & 3
        for n in range(64):
            zero = jnp.zeros((8, 128), F32)
            above = [bands[part, n - 1] if n > 0 else zero for part in range(2)]
            below = [bands[part, n + 1] if n < 63 else zero for part in range(2)]
            rim = jnp.where(
                slot < 2,
                jnp.where(slot == 0, pltpu.roll(above[0], 125, 1), pltpu.roll(below[0], 1, 1)),
                jnp.where(slot == 2, pltpu.roll(above[1], 127, 1), pltpu.roll(below[1], 3, 1)),
            )
            item = 2 * ((n & 3) * 16 + (n >> 2))
            first, second = packed(bands[0, n], bands[1, n], rim)
            out_ref[pl.ds(item, 8, stride=128), :] = first
            out_ref[pl.ds(item + 1, 8, stride=128), :] = second


def times_i(v):
    return -v[1], v[0]


def add(a, b):
    return a[0] + b[0], a[1] + b[1]


def sub(a, b):
    return a[0] - b[0], a[1] - b[1]


def times(a, c, s):
    return a[0] * c - a[1] * s, a[0] * s + a[1] * c


def four(a0, a1, a2, a3):
    p, q, m, n = add(a0, a2), add(a1, a3), sub(a0, a2), times_i(sub(a1, a3))
    return add(p, q), add(m, n), sub(p, q), sub(m, n)


def sixteen(a):
    inner = [four(a[r], a[r + 4], a[r + 8], a[r + 12]) for r in range(4)]
    out = [None] * 16
    for k in range(4):
        row = []
        for r in range(4):
            t = r * k
            v = inner[r][k]
            row.append(v if t == 0 else times(v, math.cos(math.pi * t / 8), math.sin(math.pi * t / 8)))
        for m, v in enumerate(four(*row)):
            out[k + 4 * m] = v
    return out


def row_kernel(in_ref, par_ref, row_ref, twist_ref, out_ref, x_s, a_s, b_s, power, re_s, im_s):
    d, _, _ = places()
    g = d >> 2
    for quad in range(4):
        rows = [[], [], []]
        for n in range(4):
            for half in range(2):
                start = 32 * (4 * quad + n + 16 * half)
                words = [in_ref[pl.ds(start + m, 16, stride=2), :] for m in range(2)]
                for piece, value in enumerate(unpacked(*words)):
                    rows[piece].append(value)
        for piece in range(3):
            turned = jnp.concatenate(rows[piece], axis=0).T
            for a in range(2):
                parts = swapped([turned[64 * a + 16 * n : 64 * a + 16 * n + 16] for n in range(4)], 32)
                for n, part in enumerate(parts):
                    x_s[4 * quad + n, 16 * piece : 16 * piece + 16, 128 * a : 128 * a + 128] = part
    left = pieces(x_s[...].reshape(768, HALF))
    a_s[...] = product(left, [row_ref[0, n] for n in range(PIECES)]).reshape(16, 48, HALF)
    b_s[...] = product(left, [row_ref[1, n] for n in range(PIECES)]).reshape(16, 48, HALF)
    for half in range(2):
        lanes = slice(128 * half, 128 * half + 128)
        for band in range(4):
            here = slice(8 * band, 8 * band + 8)
            values = []
            for k in range(16):
                if band < 2:
                    low = slice(16 + 8 * band, 24 + 8 * band)
                    re = a_s[k, here, lanes] - b_s[k, low, lanes]
                    im = b_s[k, here, lanes] + a_s[k, low, lanes]
                else:
                    rim = slice(16 + 8 * band, 24 + 8 * band)
                    a, b = a_s[k, rim, lanes], b_s[k, rim, lanes]
                    re = a - pltpu.roll(b, 6, 0)
                    im = b + pltpu.roll(a, 6, 0)
                values.append(times((re, im), twist_ref[0, k : k + 1, lanes], twist_ref[1, k : k + 1, lanes]))
            for k, (re, im) in enumerate(sixteen(values)):
                spot = slice(256 * k + 128 * half, 256 * k + 128 * half + 128)
                if band < 2:
                    re_s[here, spot] = re
                    im_s[here, spot] = im
                power[here, spot] = re * re + im * im
    here = power[0:16]
    rim = power[16:32]
    row = lax.broadcasted_iota(jnp.int32, (16, NX), 0)
    lane = lax.broadcasted_iota(jnp.int32, (16, NX), 1)
    up = jnp.where((row & 3) == 0, rim, pltpu.roll(here, 1, 0))
    down = jnp.where((row & 3) == 3, pltpu.roll(rim, 2, 0), pltpu.roll(here, 15, 0))

    def moved(v, offset):
        if offset > 0:
            return jnp.where(lane < NX - offset, pltpu.roll(v, NX - offset, 1), 0.0)
        return jnp.where(lane >= -offset, pltpu.roll(v, -offset, 1), 0.0)

    row_small = lax.broadcasted_iota(jnp.int32, (16, 128), 0) >> 2

    def of_rows(which):
        value = jnp.zeros((16, 128), F32)
        for n in range(4):
            value = jnp.where(row_small == n, par_ref[which, pl.ds(8 * n + g, 1), :], value)
        return value[:, 0:1]

    depth, radius, gain = of_rows(0) * (1.0 / DEPTHS), of_rows(1), of_rows(2)
    vertical = up + 2.0 * here + down
    step = down - up
    across = moved(vertical, 1) - moved(vertical, -1)
    downward = moved(step, -1) + 2.0 * step + moved(step, 1)
    energy = across * across + downward * downward
    total = energy
    for offset in range(1, MAXWIDTH + 1):
        inside = (offset <= radius).astype(F32)
        total = total + inside * (moved(energy, -offset) + moved(energy, offset))
    smoothed = total / (2.0 * radius + 1.0)
    scores = gain * jnp.log(1.0 + smoothed)
    peak = jnp.maximum(scores[0:8], scores[8:16])
    peak = jnp.maximum(peak, pltpu.roll(peak, 4, 0))
    first, second = jnp.exp(scores[0:8] - peak), jnp.exp(scores[8:16] - peak)

    def joined(v):
        return (v + pltpu.roll(v, 4, 0))[0:4]

    records = (
        peak[0:4],
        joined(first + second),
        joined(first * depth[0:8] + second * depth[8:16]),
        joined(first * re_s[0:8] + second * re_s[8:16]),
        joined(first * im_s[0:8] + second * im_s[8:16]),
    )
    for n, record in enumerate(records):
        for target in range(32):
            out_ref[target, n] = record[:, 128 * target : 128 * target + 128]


def merge_kernel(in_ref, depth_ref, focus_ref):
    for q in range(4):
        spots = [4 * g + q for g in range(8)]
        peak = in_ref[spots[0], 0]
        for n in spots[1:]:
            peak = jnp.maximum(peak, in_ref[n, 0])
        weights = [jnp.exp(in_ref[n, 0] - peak) for n in spots]
        sums = [sum(w * in_ref[n, k] for w, n in zip(weights, spots)) for k in range(1, 5)]
        rows = slice(4 * q, 4 * q + 4)
        depth_ref[rows] = sums[1] / sums[0]
        focus_ref[0, rows] = sums[2] / sums[0]
        focus_ref[1, rows] = sums[3] / sums[0]


def params(mib):
    return pltpu.CompilerParams(vmem_limit_bytes=mib * 1024 * 1024)


def whole(shape):
    return pl.BlockSpec(shape, lambda *_: (0,) * len(shape))


def cost(flops, size):
    return pl.CostEstimate(flops=flops, bytes_accessed=size, transcendentals=0)


def shards(spectrum, plane_index, kernel_width, focus_gain):
    smem = pl.BlockSpec(memory_space=pltpu.SMEM)
    picked = pl.pallas_call(
        pick_kernel,
        in_specs=[smem, smem, smem, pl.BlockSpec(memory_space=pl.ANY)],
        out_specs=whole((32, 24, 128)),
        out_shape=jax.ShapeDtypeStruct((32, 24, 128), BF16),
        scratch_shapes=[pltpu.VMEM((2, 128, 256), BF16), pltpu.SemaphoreType.DMA(())],
        compiler_params=params(58),
        cost_estimate=cost(50_000_000, 300_000),
        name="pick",
    )(plane_index, kernel_width, focus_gain, spectrum)
    groups = [[16 * d + (d + j) % 16 for d in range(32)] for j in range(16)]
    columns = lax.all_to_all(
        picked, ALL, split_axis=0, concat_axis=0, tiled=True, axis_index_groups=groups
    )

    tables, row_table, twist = pl.pallas_call(
        table_kernel,
        grid=(BLOCKS,),
        in_specs=[],
        out_specs=[
            pl.BlockSpec((1, 2, PIECES, HALF, HALF), lambda b: (b, 0, 0, 0, 0)),
            whole((2, PIECES, HALF, HALF)),
            whole((2, 16, HALF)),
        ],
        out_shape=[
            jax.ShapeDtypeStruct((BLOCKS, 2, PIECES, HALF, HALF), BF16),
            jax.ShapeDtypeStruct((2, PIECES, HALF, HALF), BF16),
            jax.ShapeDtypeStruct((2, 16, HALF), F32),
        ],
        scratch_shapes=[pltpu.VMEM((HALF, HALF), F32), pltpu.VMEM((HALF, HALF), F32)],
        compiler_params=params(16),
        cost_estimate=cost(30_000_000, 5_000_000),
        name="tables",
    )()

    messages, planes = pl.pallas_call(
        column_kernel,
        grid=(BLOCKS,),
        in_specs=[
            whole((32, 24, 128)),
            pl.BlockSpec((1, 2, PIECES, HALF, HALF), lambda b: (b, 0, 0, 0, 0)),
        ],
        out_specs=[whole((1024, 128)), whole((3, 32, 128))],
        out_shape=[
            jax.ShapeDtypeStruct((1024, 128), jnp.int32),
            jax.ShapeDtypeStruct((3, 32, 128), F32),
        ],
        scratch_shapes=[
            pltpu.VMEM((2, HALF, HALF), F32),
            pltpu.VMEM((256, 128), F32),
            pltpu.VMEM((2, 64, 8, 128), F32),
        ],
        compiler_params=params(50),
        cost_estimate=cost(6_500_000_000, 8_000_000),
        name="columns",
    )(columns, tables)
    arrived = lax.all_to_all(
        messages.reshape(512, 1, 256), ALL, split_axis=0, concat_axis=0, tiled=True
    )

    records = pl.pallas_call(
        row_kernel,
        in_specs=[
            whole((1024, 128)),
            whole((3, 32, 128)),
            whole((2, PIECES, HALF, HALF)),
            whole((2, 16, HALF)),
        ],
        out_specs=whole((32, 5, 4, 128)),
        out_shape=jax.ShapeDtypeStruct((32, 5, 4, 128), F32),
        scratch_shapes=[
            pltpu.VMEM((16, 48, HALF), F32),
            pltpu.VMEM((16, 48, HALF), F32),
            pltpu.VMEM((16, 48, HALF), F32),
            pltpu.VMEM((32, NX), F32),
            pltpu.VMEM((16, NX), F32),
            pltpu.VMEM((16, NX), F32),
        ],
        compiler_params=params(24),
        cost_estimate=cost(1_000_000_000, 2_200_000),
        name="rows",
    )(arrived.reshape(1024, 128), planes, row_table, twist)
    merged = lax.all_to_all(records, "depth", split_axis=0, concat_axis=0, tiled=True)

    depth_map, focused = pl.pallas_call(
        merge_kernel,
        in_specs=[whole((32, 5, 4, 128))],
        out_specs=[whole((16, 128)), whole((2, 16, 128))],
        out_shape=[
            jax.ShapeDtypeStruct((16, 128), F32),
            jax.ShapeDtypeStruct((2, 16, 128), F32),
        ],
        compiler_params=params(4),
        cost_estimate=cost(1_000_000, 500_000),
        name="merge",
    )(merged)
    return depth_map, focused


def solution(mesh):
    return jax.shard_map(
        shards,
        mesh=mesh,
        in_specs=(P(None, "rows", None), P("depth"), P("depth"), P("depth")),
        out_specs=(P("rows", "depth"), P(None, "rows", "depth")),
        check_vma=False,
    )
```

```python
import math

import jax
import jax.numpy as jnp
from jax import lax
from jax.experimental import pallas as pl
from jax.experimental.pallas import tpu as pltpu
from jax.sharding import PartitionSpec as P

NX = 4096
Y_WIN = 256
DEPTHS = 2048
MAXWIDTH = 3
TURN = NX * NX
HALF = 256
BLOCKS = 8
F32 = jnp.float32
BF16 = jnp.bfloat16
PIECES = 2
ALL = ("depth", "rows")


def cos_sin(turns):
    quarter = (turns + (1 << 21)) >> 22
    rest = turns - (quarter << 22)
    x = rest.astype(F32) * (2.0 * math.pi / TURN)
    x2 = x * x
    s = x * (1.0 + x2 * (-1.0 / 6 + x2 * (1.0 / 120 + x2 * (-1.0 / 5040 + x2 * (1.0 / 362880)))))
    c = 1.0 + x2 * (-0.5 + x2 * (1.0 / 24 + x2 * (-1.0 / 720 + x2 * (1.0 / 40320 - x2 * (1.0 / 3628800)))))
    odd = (quarter & 1) == 1
    cos_v = jnp.where(odd, s, c)
    sin_v = jnp.where(odd, c, s)
    cos_v = jnp.where(((quarter + 1) & 2) == 2, -cos_v, cos_v)
    sin_v = jnp.where((quarter & 2) == 2, -sin_v, sin_v)
    return cos_v, sin_v


def chirp_turns(z, s):
    square = s * s
    return (z * (square & (NX - 1)) + NX * ((z * (square >> 12)) & (NX - 1))) & (TURN - 1)


def pieces(value):
    out = []
    for n in range(PIECES):
        out.append(value.astype(BF16))
        if n < PIECES - 1:
            value = value - out[-1].astype(F32)
    return out


def dot(a, b):
    return jnp.dot(a, b, preferred_element_type=F32)


def product(left, right):
    if PIECES == 2:
        return (dot(left[0], right[1]) + dot(left[1], right[0])) + dot(left[0], right[0])
    return (
        (dot(left[0], right[2]) + dot(left[2], right[0]) + dot(left[1], right[1]))
        + (dot(left[0], right[1]) + dot(left[1], right[0]))
        + dot(left[0], right[0])
    )


def places():
    d, r = lax.axis_index("depth"), lax.axis_index("rows")
    return d, r, (r - d) & 15


def swapped(parts, group):
    count = len(parts)
    lane = lax.broadcasted_iota(jnp.int32, parts[0].shape, 1)
    parts = list(parts)
    step = 1
    while step < count:
        low = ((lane // group) & step) == 0
        for i in range(count):
            if i & step == 0:
                x, y = parts[i], parts[i + step]
                parts[i] = jnp.where(low, x, pltpu.roll(y, group * step, 1))
                parts[i + step] = jnp.where(low, pltpu.roll(x, 128 - group * step, 1), y)
        step *= 2
    return parts


def packed(re, im, rim):
    most = jnp.maximum(jnp.maximum(jnp.abs(re), jnp.abs(im)), jnp.abs(rim))
    small = most < 2.0**-40
    lift = jnp.where(small, 2.0**80, 1.0)
    power = jnp.floor(jnp.log2(jnp.maximum(most * lift, 2.0**-46)) + 0.01).astype(jnp.int32) + 1
    scale = jnp.exp2((18 - power).astype(F32)) * lift

    def whole_number(v):
        return jnp.floor(v + 0.5).astype(jnp.int32)

    a, b, c = whole_number(re * scale), whole_number(im * scale), whole_number(rim * scale * 0.5)
    code = power + jnp.where(small, 128 - 80, 128)
    first = (a << 13) | (code << 5) | (c & 31)
    second = (b << 13) | ((c >> 5) & 0x1FFF)
    return first, second


def unpacked(first, second):
    power = ((first >> 5) & 255) - 128
    small = power < -40
    scale = jnp.exp2((jnp.where(small, power + 80, power) - 18).astype(F32))
    scale = scale * jnp.where(small, 2.0**-80, 1.0)
    c = (((second << 19) >> 19) << 5) + (first & 31)
    return (first >> 13).astype(F32) * scale, (second >> 13).astype(F32) * scale, c.astype(F32) * (scale * 2.0)


def pick_kernel(z_ref, width_ref, gain_ref, spec_ref, out_ref, buf, sem):
    d, r, j = places()
    copy = pltpu.make_async_copy(
        spec_ref.at[:, pl.ds(pl.multiple_of(128 * (d >> 4), 128), 128), pl.ds(pl.multiple_of(256 * j, 256), 256)],
        buf,
        sem,
    )
    copy.start()
    q = lax.broadcasted_iota(jnp.int32, (256, 256), 0)
    lane = lax.broadcasted_iota(jnp.int32, (256, 256), 1)
    target = q >> 3
    sort = (lane == (target & 15) + 128 * (target >> 4) + 16 * (q & 7)).astype(F32).astype(BF16)
    i = lax.broadcasted_iota(jnp.int32, (128, 128), 0)
    l = lax.broadcasted_iota(jnp.int32, (128, 128), 1)
    source = jnp.where(r < BLOCKS, l, (128 - l) & 127)
    turn = (i == source).astype(F32).astype(BF16)
    row = lax.broadcasted_iota(jnp.int32, (8, 128), 0)
    gain = jnp.full((8, 128), gain_ref[0], F32)
    high = gain.astype(BF16).astype(F32)
    mid = (gain - high).astype(BF16).astype(F32)
    z = z_ref[0]
    extra = jnp.zeros((8, 128), F32)
    values = ((z & ~31).astype(F32), (z & 31).astype(F32), width_ref[0].astype(F32), high, mid, gain - high - mid)
    for n, value in enumerate(values):
        extra = jnp.where(row == n, value, extra)
    copy.wait()
    both = []
    for c in range(2):
        picked = lax.dot_general(sort, buf[c], (((1,), (1,)), ((), ())), preferred_element_type=F32)
        both.append(dot(picked.astype(BF16), turn).reshape(32, 8, 128))
    both.append(jnp.broadcast_to(extra[None], (32, 8, 128)))
    out_ref[...] = jnp.concatenate(both, axis=1).astype(BF16)


def table_kernel(high_ref, low_ref, row_ref, twist_ref, base_c, base_s):
    b = pl.program_id(0)
    l = lax.broadcasted_iota(jnp.int32, (HALF, HALF), 0)
    y = lax.broadcasted_iota(jnp.int32, (HALF, HALF), 1)

    @pl.when(b == 0)
    def _():
        c, s = cos_sin((l * y & (NX - 1)) << 12)
        base_c[...] = c
        base_s[...] = s
        number = 16 * (l & 15) + 8 * ((l >> 4) & 1) + 4 * (l >> 7) + ((l >> 5) & 3)
        c, s = cos_sin((number * y & 255) << 16)
        for n, part in enumerate(pieces(c)):
            row_ref[0, n] = part
        for n, part in enumerate(pieces(s)):
            row_ref[1, n] = part
        k = lax.broadcasted_iota(jnp.int32, (16, HALF), 0)
        x = lax.broadcasted_iota(jnp.int32, (16, HALF), 1)
        c, s = cos_sin(((k * x - 256 * k * x) & (NX - 1)) << 12)
        twist_ref[0] = c * (1.0 / NX)
        twist_ref[1] = s * (1.0 / NX)

    lane = lax.broadcasted_iota(jnp.int32, (8, HALF), 1)
    c16, s16 = cos_sin((b * lane & 15) << 20)
    c16, s16 = c16[0:1], s16[0:1]
    cosine = base_c[...] * c16 - base_s[...] * s16
    sine = base_s[...] * c16 + base_c[...] * s16
    nyquist = (1 - 2 * (y & 1)).astype(F32)
    sine = jnp.where((l == 0) & (b == 0), nyquist, sine)
    for t, value in enumerate((cosine, sine)):
        high_ref[0, t], low_ref[0, t] = pieces(value)


def column_kernel(spec_ref, high_ref, low_hbm, out_ref, par_ref, acc, par_s, bands, low_s, sems):
    d, r, j = places()

    def fetch(n):
        return pltpu.make_async_copy(low_hbm.at[n], low_s.at[n], sems.at[n])

    for n in range(BLOCKS):
        fetch(n).start()
    par_s[...] = spec_ref[:, 16:24].astype(F32).reshape(256, 128)
    rows = [par_s[pl.ds(n, 32, stride=8), :] for n in range(6)]
    par_ref[0] = rows[0] + rows[1]
    par_ref[1] = rows[2]
    par_ref[2] = rows[3] + rows[4] + rows[5]
    z = par_ref[0].astype(jnp.int32)
    acc[...] = jnp.zeros_like(acc)

    def step(b, carry):
        fetch(b).wait()
        lane = lax.broadcasted_iota(jnp.int32, (32, HALF), 1)
        special = (lane == 0) & (b == 0)
        z2 = jnp.concatenate([z, z], axis=1)
        s = jnp.where(special, NX // 2, b * HALF + lane)
        c_o, s_o = cos_sin(chirp_turns(z2, s))
        s_o = -s_o
        c_e = jnp.where(special, 1.0, c_o)
        s_e = jnp.where(special, 0.0, s_o)

        def block(n):
            return spec_ref[(((n >> 1) - j) & 15) + 16 * (n & 1), 0:16].astype(F32)

        lane16 = lax.broadcasted_iota(jnp.int32, (16, HALF), 1)
        plus = jnp.concatenate([block(2 * b), block(2 * b + 1)], axis=1)
        middle = block(31 - 2 * b)
        last = jnp.concatenate([middle, block(30 - 2 * b)], axis=1)
        first = jnp.concatenate([block(jnp.where(b == 0, 16, 32 - 2 * b)), middle], axis=1)
        minus = jnp.where((lane16 & 127) == 0, first, last)
        corner = (lane16 == 0) & (b == 0)
        even = jnp.where(corner, plus, plus + minus)
        odd = plus - minus
        o_re = jnp.where(corner[:8], minus[:8], -odd[8:])
        o_im = jnp.where(corner[:8], minus[8:], odd[:8])
        e_re, e_im = even[:8], even[8:]

        def turned(re, im, c, s):
            re, im = re[:, None, :], im[:, None, :]
            t_re = (re * c[None] - im * s[None]).reshape(HALF, HALF)
            t_im = (re * s[None] + im * c[None]).reshape(HALF, HALF)
            return t_re, t_im

        parts = []
        for t, (re, im, c, s) in enumerate(((e_re, e_im, c_e, s_e), (o_re, o_im, c_o, s_o))):
            for value in turned(re, im, c, s):
                parts.append(product(pieces(value), [high_ref[b, t], low_s[b, t]]))
        for half in range(2):
            acc[half] += parts[half] + parts[half + 2]
        return carry

    lax.fori_loop(0, BLOCKS, step, 0, unroll=4)
    lane = lax.broadcasted_iota(jnp.int32, (8, 128), 1)
    group = (lane >> 2) & 3
    plane = z[0:8]
    for n in range(1, 4):
        plane = jnp.where(group == n, z[8 * n : 8 * n + 8], plane)
    v = 256 * j + 128 * (d >> 4) + 16 * (lane >> 4) + (d & 15)
    c, s = cos_sin(chirp_turns(plane, jnp.where(v < NX // 2, v, v - NX)))
    s = -s
    for half in range(2):
        cols = slice(128 * half, 128 * half + 128)
        for part in range(2):
            for n, v in enumerate(swapped([acc[part, 8 * i : 8 * i + 8, cols] for i in range(32)], 4)):
                bands[part, 32 * half + n] = v
    for n in range(64):
        re, im = bands[0, n], bands[1, n]
        bands[0, n] = re * c - im * s
        bands[1, n] = re * s + im * c
    slot = lane & 3
    for n in range(64):
        zero = jnp.zeros((8, 128), F32)
        above = [bands[part, n - 1] if n > 0 else zero for part in range(2)]
        below = [bands[part, n + 1] if n < 63 else zero for part in range(2)]
        rim = jnp.where(
            slot < 2,
            jnp.where(slot == 0, pltpu.roll(above[0], 125, 1), pltpu.roll(below[0], 1, 1)),
            jnp.where(slot == 2, pltpu.roll(above[1], 127, 1), pltpu.roll(below[1], 3, 1)),
        )
        item = 2 * ((n & 3) * 16 + (n >> 2))
        first, second = packed(bands[0, n], bands[1, n], rim)
        out_ref[pl.ds(item, 8, stride=128), :] = first
        out_ref[pl.ds(item + 1, 8, stride=128), :] = second


def times_i(v):
    return -v[1], v[0]


def add(a, b):
    return a[0] + b[0], a[1] + b[1]


def sub(a, b):
    return a[0] - b[0], a[1] - b[1]


def times(a, c, s):
    return a[0] * c - a[1] * s, a[0] * s + a[1] * c


def four(a0, a1, a2, a3):
    p, q, m, n = add(a0, a2), add(a1, a3), sub(a0, a2), times_i(sub(a1, a3))
    return add(p, q), add(m, n), sub(p, q), sub(m, n)


def sixteen(a):
    inner = [four(a[r], a[r + 4], a[r + 8], a[r + 12]) for r in range(4)]
    out = [None] * 16
    for k in range(4):
        row = []
        for r in range(4):
            t = r * k
            v = inner[r][k]
            row.append(v if t == 0 else times(v, math.cos(math.pi * t / 8), math.sin(math.pi * t / 8)))
        for m, v in enumerate(four(*row)):
            out[k + 4 * m] = v
    return out


def row_kernel(in_ref, par_ref, row_ref, twist_ref, out_ref, x_s, a_s, b_s, power, re_s, im_s):
    d, _, _ = places()
    g = d >> 2
    for quad in range(4):
        rows = [[], [], []]
        for n in range(4):
            for half in range(2):
                start = 32 * (4 * quad + n + 16 * half)
                words = [in_ref[pl.ds(start + m, 16, stride=2), :] for m in range(2)]
                for piece, value in enumerate(unpacked(*words)):
                    rows[piece].append(value)
        for piece in range(3):
            turned = jnp.concatenate(rows[piece], axis=0).T
            for a in range(2):
                parts = swapped([turned[64 * a + 16 * n : 64 * a + 16 * n + 16] for n in range(4)], 32)
                for n, part in enumerate(parts):
                    x_s[4 * quad + n, 16 * piece : 16 * piece + 16, 128 * a : 128 * a + 128] = part
    left = pieces(x_s[...].reshape(768, HALF))
    a_s[...] = product(left, [row_ref[0, n] for n in range(PIECES)]).reshape(16, 48, HALF)
    b_s[...] = product(left, [row_ref[1, n] for n in range(PIECES)]).reshape(16, 48, HALF)
    for half in range(2):
        lanes = slice(128 * half, 128 * half + 128)
        for band in range(4):
            here = slice(8 * band, 8 * band + 8)
            values = []
            for k in range(16):
                if band < 2:
                    low = slice(16 + 8 * band, 24 + 8 * band)
                    re = a_s[k, here, lanes] - b_s[k, low, lanes]
                    im = b_s[k, here, lanes] + a_s[k, low, lanes]
                else:
                    rim = slice(16 + 8 * band, 24 + 8 * band)
                    a, b = a_s[k, rim, lanes], b_s[k, rim, lanes]
                    re = a - pltpu.roll(b, 6, 0)
                    im = b + pltpu.roll(a, 6, 0)
                values.append(times((re, im), twist_ref[0, k : k + 1, lanes], twist_ref[1, k : k + 1, lanes]))
            for k, (re, im) in enumerate(sixteen(values)):
                spot = slice(256 * k + 128 * half, 256 * k + 128 * half + 128)
                if band < 2:
                    re_s[here, spot] = re
                    im_s[here, spot] = im
                power[here, spot] = re * re + im * im
    here = power[0:16]
    rim = power[16:32]
    row = lax.broadcasted_iota(jnp.int32, (16, NX), 0)
    lane = lax.broadcasted_iota(jnp.int32, (16, NX), 1)
    up = jnp.where((row & 3) == 0, rim, pltpu.roll(here, 1, 0))
    down = jnp.where((row & 3) == 3, pltpu.roll(rim, 2, 0), pltpu.roll(here, 15, 0))

    def moved(v, offset):
        if offset > 0:
            return jnp.where(lane < NX - offset, pltpu.roll(v, NX - offset, 1), 0.0)
        return jnp.where(lane >= -offset, pltpu.roll(v, -offset, 1), 0.0)

    row_small = lax.broadcasted_iota(jnp.int32, (16, 128), 0) >> 2

    def of_rows(which):
        value = jnp.zeros((16, 128), F32)
        for n in range(4):
            value = jnp.where(row_small == n, par_ref[which, pl.ds(8 * n + g, 1), :], value)
        return value[:, 0:1]

    depth, radius, gain = of_rows(0) * (1.0 / DEPTHS), of_rows(1), of_rows(2)
    vertical = up + 2.0 * here + down
    step = down - up
    across = moved(vertical, 1) - moved(vertical, -1)
    downward = moved(step, -1) + 2.0 * step + moved(step, 1)
    energy = across * across + downward * downward
    total = energy
    for offset in range(1, MAXWIDTH + 1):
        inside = (offset <= radius).astype(F32)
        total = total + inside * (moved(energy, -offset) + moved(energy, offset))
    smoothed = total / (2.0 * radius + 1.0)
    scores = gain * jnp.log(1.0 + smoothed)
    peak = jnp.maximum(scores[0:8], scores[8:16])
    peak = jnp.maximum(peak, pltpu.roll(peak, 4, 0))
    first, second = jnp.exp(scores[0:8] - peak), jnp.exp(scores[8:16] - peak)

    def joined(v):
        return (v + pltpu.roll(v, 4, 0))[0:4]

    records = (
        peak[0:4],
        joined(first + second),
        joined(first * depth[0:8] + second * depth[8:16]),
        joined(first * re_s[0:8] + second * re_s[8:16]),
        joined(first * im_s[0:8] + second * im_s[8:16]),
    )
    for n, record in enumerate(records):
        for target in range(32):
            out_ref[target, n] = record[:, 128 * target : 128 * target + 128]


def merge_kernel(in_ref, depth_ref, focus_ref):
    for q in range(4):
        spots = [4 * g + q for g in range(8)]
        peak = in_ref[spots[0], 0]
        for n in spots[1:]:
            peak = jnp.maximum(peak, in_ref[n, 0])
        weights = [jnp.exp(in_ref[n, 0] - peak) for n in spots]
        sums = [sum(w * in_ref[n, k] for w, n in zip(weights, spots)) for k in range(1, 5)]
        rows = slice(4 * q, 4 * q + 4)
        depth_ref[rows] = sums[1] / sums[0]
        focus_ref[0, rows] = sums[2] / sums[0]
        focus_ref[1, rows] = sums[3] / sums[0]


def params(mib):
    return pltpu.CompilerParams(vmem_limit_bytes=mib * 1024 * 1024)


def whole(shape):
    return pl.BlockSpec(shape, lambda *_: (0,) * len(shape))


def cost(flops, size):
    return pl.CostEstimate(flops=flops, bytes_accessed=size, transcendentals=0)


def shards(spectrum, plane_index, kernel_width, focus_gain):
    smem = pl.BlockSpec(memory_space=pltpu.SMEM)
    picked = pl.pallas_call(
        pick_kernel,
        in_specs=[smem, smem, smem, pl.BlockSpec(memory_space=pl.ANY)],
        out_specs=whole((32, 24, 128)),
        out_shape=jax.ShapeDtypeStruct((32, 24, 128), BF16),
        scratch_shapes=[pltpu.VMEM((2, 128, 256), BF16), pltpu.SemaphoreType.DMA(())],
        compiler_params=params(58),
        cost_estimate=cost(50_000_000, 300_000),
        name="pick",
    )(plane_index, kernel_width, focus_gain, spectrum)
    groups = [[16 * d + (d + j) % 16 for d in range(32)] for j in range(16)]
    columns = lax.all_to_all(
        picked, ALL, split_axis=0, concat_axis=0, tiled=True, axis_index_groups=groups
    )

    high, low, row_table, twist = pl.pallas_call(
        table_kernel,
        grid=(BLOCKS,),
        in_specs=[],
        out_specs=[
            pl.BlockSpec((1, 2, HALF, HALF), lambda b: (b, 0, 0, 0)),
            pl.BlockSpec((1, 2, HALF, HALF), lambda b: (b, 0, 0, 0)),
            whole((2, PIECES, HALF, HALF)),
            whole((2, 16, HALF)),
        ],
        out_shape=[
            jax.ShapeDtypeStruct((BLOCKS, 2, HALF, HALF), BF16),
            jax.ShapeDtypeStruct((BLOCKS, 2, HALF, HALF), BF16),
            jax.ShapeDtypeStruct((2, PIECES, HALF, HALF), BF16),
            jax.ShapeDtypeStruct((2, 16, HALF), F32),
        ],
        scratch_shapes=[pltpu.VMEM((HALF, HALF), F32), pltpu.VMEM((HALF, HALF), F32)],
        compiler_params=params(16),
        cost_estimate=cost(30_000_000, 5_000_000),
        name="tables",
    )()

    messages, planes = pl.pallas_call(
        column_kernel,
        in_specs=[
            whole((32, 24, 128)),
            whole((BLOCKS, 2, HALF, HALF)),
            pl.BlockSpec(memory_space=pl.ANY),
        ],
        out_specs=[whole((1024, 128)), whole((3, 32, 128))],
        out_shape=[
            jax.ShapeDtypeStruct((1024, 128), jnp.int32),
            jax.ShapeDtypeStruct((3, 32, 128), F32),
        ],
        scratch_shapes=[
            pltpu.VMEM((2, HALF, HALF), F32),
            pltpu.VMEM((256, 128), F32),
            pltpu.VMEM((2, 64, 8, 128), F32),
            pltpu.VMEM((BLOCKS, 2, HALF, HALF), BF16),
            pltpu.SemaphoreType.DMA((BLOCKS,)),
        ],
        compiler_params=params(50),
        cost_estimate=cost(6_500_000_000, 8_000_000),
        name="columns",
    )(columns, high, low)
    arrived = lax.all_to_all(
        messages.reshape(512, 1, 256), ALL, split_axis=0, concat_axis=0, tiled=True
    )

    records = pl.pallas_call(
        row_kernel,
        in_specs=[
            whole((1024, 128)),
            whole((3, 32, 128)),
            whole((2, PIECES, HALF, HALF)),
            whole((2, 16, HALF)),
        ],
        out_specs=whole((32, 5, 4, 128)),
        out_shape=jax.ShapeDtypeStruct((32, 5, 4, 128), F32),
        scratch_shapes=[
            pltpu.VMEM((16, 48, HALF), F32),
            pltpu.VMEM((16, 48, HALF), F32),
            pltpu.VMEM((16, 48, HALF), F32),
            pltpu.VMEM((32, NX), F32),
            pltpu.VMEM((16, NX), F32),
            pltpu.VMEM((16, NX), F32),
        ],
        compiler_params=params(24),
        cost_estimate=cost(1_000_000_000, 2_200_000),
        name="rows",
    )(arrived.reshape(1024, 128), planes, row_table, twist)
    merged = lax.all_to_all(records, "depth", split_axis=0, concat_axis=0, tiled=True)

    depth_map, focused = pl.pallas_call(
        merge_kernel,
        in_specs=[whole((32, 5, 4, 128))],
        out_specs=[whole((16, 128)), whole((2, 16, 128))],
        out_shape=[
            jax.ShapeDtypeStruct((16, 128), F32),
            jax.ShapeDtypeStruct((2, 16, 128), F32),
        ],
        compiler_params=params(4),
        cost_estimate=cost(1_000_000, 500_000),
        name="merge",
    )(merged)
    return depth_map, focused


def solution(mesh):
    return jax.shard_map(
        shards,
        mesh=mesh,
        in_specs=(P(None, "rows", None), P("depth"), P("depth"), P("depth")),
        out_specs=(P("rows", "depth"), P(None, "rows", "depth")),
        check_vma=False,
    )
```

```python
import math

import jax
import jax.numpy as jnp
from jax import lax
from jax.experimental import pallas as pl
from jax.experimental.pallas import tpu as pltpu
from jax.sharding import PartitionSpec as P

NX = 4096
Y_WIN = 256
DEPTHS = 2048
MAXWIDTH = 3
TURN = NX * NX
HALF = 256
BLOCKS = 8
F32 = jnp.float32
BF16 = jnp.bfloat16
PIECES = 2
ALL = ("depth", "rows")


def cos_sin(turns):
    quarter = (turns + (1 << 21)) >> 22
    rest = turns - (quarter << 22)
    x = rest.astype(F32) * (2.0 * math.pi / TURN)
    x2 = x * x
    s = x * (1.0 + x2 * (-1.0 / 6 + x2 * (1.0 / 120 + x2 * (-1.0 / 5040 + x2 * (1.0 / 362880)))))
    c = 1.0 + x2 * (-0.5 + x2 * (1.0 / 24 + x2 * (-1.0 / 720 + x2 * (1.0 / 40320 - x2 * (1.0 / 3628800)))))
    odd = (quarter & 1) == 1
    cos_v = jnp.where(odd, s, c)
    sin_v = jnp.where(odd, c, s)
    cos_v = jnp.where(((quarter + 1) & 2) == 2, -cos_v, cos_v)
    sin_v = jnp.where((quarter & 2) == 2, -sin_v, sin_v)
    return cos_v, sin_v


def chirp_turns(z, s):
    square = s * s
    return (z * (square & (NX - 1)) + NX * ((z * (square >> 12)) & (NX - 1))) & (TURN - 1)


def pieces(value):
    out = []
    for n in range(PIECES):
        out.append(value.astype(BF16))
        if n < PIECES - 1:
            value = value - out[-1].astype(F32)
    return out


def dot(a, b):
    return jnp.dot(a, b, preferred_element_type=F32)


def product(left, right):
    if PIECES == 2:
        return (dot(left[0], right[1]) + dot(left[1], right[0])) + dot(left[0], right[0])
    return (
        (dot(left[0], right[2]) + dot(left[2], right[0]) + dot(left[1], right[1]))
        + (dot(left[0], right[1]) + dot(left[1], right[0]))
        + dot(left[0], right[0])
    )


def places():
    d, r = lax.axis_index("depth"), lax.axis_index("rows")
    return d, r, (r - d) & 15


def swapped(parts, group):
    count = len(parts)
    lane = lax.broadcasted_iota(jnp.int32, parts[0].shape, 1)
    parts = list(parts)
    step = 1
    while step < count:
        low = ((lane // group) & step) == 0
        for i in range(count):
            if i & step == 0:
                x, y = parts[i], parts[i + step]
                parts[i] = jnp.where(low, x, pltpu.roll(y, group * step, 1))
                parts[i + step] = jnp.where(low, pltpu.roll(x, 128 - group * step, 1), y)
        step *= 2
    return parts


def packed(re, im, rim):
    most = jnp.maximum(jnp.maximum(jnp.abs(re), jnp.abs(im)), jnp.abs(rim))
    small = most < 2.0**-40
    lift = jnp.where(small, 2.0**80, 1.0)
    power = jnp.floor(jnp.log2(jnp.maximum(most * lift, 2.0**-46)) + 0.01).astype(jnp.int32) + 1
    scale = jnp.exp2((18 - power).astype(F32)) * lift

    def whole_number(v):
        return jnp.floor(v + 0.5).astype(jnp.int32)

    a, b, c = whole_number(re * scale), whole_number(im * scale), whole_number(rim * scale * 0.5)
    code = power + jnp.where(small, 128 - 80, 128)
    first = (a << 13) | (code << 5) | (c & 31)
    second = (b << 13) | ((c >> 5) & 0x1FFF)
    return first, second


def unpacked(first, second):
    power = ((first >> 5) & 255) - 128
    small = power < -40
    scale = jnp.exp2((jnp.where(small, power + 80, power) - 18).astype(F32))
    scale = scale * jnp.where(small, 2.0**-80, 1.0)
    c = (((second << 19) >> 19) << 5) + (first & 31)
    return (first >> 13).astype(F32) * scale, (second >> 13).astype(F32) * scale, c.astype(F32) * (scale * 2.0)


def pick_kernel(z_ref, width_ref, gain_ref, spec_ref, out_ref, buf, sem):
    d, r, j = places()
    copy = pltpu.make_async_copy(
        spec_ref.at[:, pl.ds(pl.multiple_of(128 * (d >> 4), 128), 128), pl.ds(pl.multiple_of(256 * j, 256), 256)],
        buf,
        sem,
    )
    copy.start()
    q = lax.broadcasted_iota(jnp.int32, (256, 256), 0)
    lane = lax.broadcasted_iota(jnp.int32, (256, 256), 1)
    target = q >> 3
    sort = (lane == (target & 15) + 128 * (target >> 4) + 16 * (q & 7)).astype(F32).astype(BF16)
    i = lax.broadcasted_iota(jnp.int32, (128, 128), 0)
    l = lax.broadcasted_iota(jnp.int32, (128, 128), 1)
    source = jnp.where(r < BLOCKS, l, (128 - l) & 127)
    turn = (i == source).astype(F32).astype(BF16)
    row = lax.broadcasted_iota(jnp.int32, (8, 128), 0)
    gain = jnp.full((8, 128), gain_ref[0], F32)
    high = gain.astype(BF16).astype(F32)
    mid = (gain - high).astype(BF16).astype(F32)
    z = z_ref[0]
    extra = jnp.zeros((8, 128), F32)
    values = ((z & ~31).astype(F32), (z & 31).astype(F32), width_ref[0].astype(F32), high, mid, gain - high - mid)
    for n, value in enumerate(values):
        extra = jnp.where(row == n, value, extra)
    copy.wait()
    both = []
    for c in range(2):
        picked = lax.dot_general(sort, buf[c], (((1,), (1,)), ((), ())), preferred_element_type=F32)
        both.append(dot(picked.astype(BF16), turn).reshape(32, 8, 128))
    both.append(jnp.broadcast_to(extra[None], (32, 8, 128)))
    out_ref[...] = jnp.concatenate(both, axis=1).astype(BF16)


def table_kernel(high_ref, low_ref, row_ref, twist_ref, base_c, base_s):
    b = pl.program_id(0)
    l = lax.broadcasted_iota(jnp.int32, (HALF, HALF), 0)
    y = lax.broadcasted_iota(jnp.int32, (HALF, HALF), 1)

    @pl.when(b == 0)
    def _():
        c, s = cos_sin((l * y & (NX - 1)) << 12)
        base_c[...] = c
        base_s[...] = s
        number = 16 * (l & 15) + 8 * ((l >> 4) & 1) + 4 * (l >> 7) + ((l >> 5) & 3)
        c, s = cos_sin((number * y & 255) << 16)
        for n, part in enumerate(pieces(c)):
            row_ref[0, n] = part
        for n, part in enumerate(pieces(s)):
            row_ref[1, n] = part
        k = lax.broadcasted_iota(jnp.int32, (16, HALF), 0)
        x = lax.broadcasted_iota(jnp.int32, (16, HALF), 1)
        c, s = cos_sin(((k * x - 256 * k * x) & (NX - 1)) << 12)
        twist_ref[0] = c * (1.0 / NX)
        twist_ref[1] = s * (1.0 / NX)

    lane = lax.broadcasted_iota(jnp.int32, (8, HALF), 1)
    c16, s16 = cos_sin((b * lane & 15) << 20)
    c16, s16 = c16[0:1], s16[0:1]
    cosine = base_c[...] * c16 - base_s[...] * s16
    sine = base_s[...] * c16 + base_c[...] * s16
    nyquist = (1 - 2 * (y & 1)).astype(F32)
    sine = jnp.where((l == 0) & (b == 0), nyquist, sine)
    for t, value in enumerate((cosine, sine)):
        high_ref[0, t], low_ref[0, t] = pieces(value)


def column_kernel(spec_ref, high_ref, low_hbm, out_ref, par_ref, acc, par_s, bands, low_s, sems):
    d, r, j = places()

    def fetch(n):
        return pltpu.make_async_copy(low_hbm.at[n], low_s.at[n], sems.at[n])

    for n in range(BLOCKS):
        fetch(n).start()
    par_s[...] = spec_ref[:, 16:24].astype(F32).reshape(256, 128)
    rows = [par_s[pl.ds(n, 32, stride=8), :] for n in range(6)]
    par_ref[0] = rows[0] + rows[1]
    par_ref[1] = rows[2]
    par_ref[2] = rows[3] + rows[4] + rows[5]
    z = par_ref[0].astype(jnp.int32)
    acc[...] = jnp.zeros_like(acc)

    def step(b, carry):
        fetch(b).wait()
        lane = lax.broadcasted_iota(jnp.int32, (32, HALF), 1)
        special = (lane == 0) & (b == 0)
        z2 = jnp.concatenate([z, z], axis=1)
        s = jnp.where(special, NX // 2, b * HALF + lane)
        c_o, s_o = cos_sin(chirp_turns(z2, s))
        s_o = -s_o
        c_e = jnp.where(special, 1.0, c_o)
        s_e = jnp.where(special, 0.0, s_o)

        def block(n):
            return spec_ref[(((n >> 1) - j) & 15) + 16 * (n & 1), 0:16].astype(F32)

        lane16 = lax.broadcasted_iota(jnp.int32, (16, HALF), 1)
        plus = jnp.concatenate([block(2 * b), block(2 * b + 1)], axis=1)
        middle = block(31 - 2 * b)
        last = jnp.concatenate([middle, block(30 - 2 * b)], axis=1)
        first = jnp.concatenate([block(jnp.where(b == 0, 16, 32 - 2 * b)), middle], axis=1)
        minus = jnp.where((lane16 & 127) == 0, first, last)
        corner = (lane16 == 0) & (b == 0)
        even = jnp.where(corner, plus, plus + minus)
        odd = plus - minus
        o_re = jnp.where(corner[:8], minus[:8], -odd[8:])
        o_im = jnp.where(corner[:8], minus[8:], odd[:8])
        e_re, e_im = even[:8], even[8:]

        def turned(re, im, c, s):
            re, im = re[:, None, :], im[:, None, :]
            t_re = (re * c[None] - im * s[None]).reshape(HALF, HALF)
            t_im = (re * s[None] + im * c[None]).reshape(HALF, HALF)
            return t_re, t_im

        parts = []
        for t, (re, im, c, s) in enumerate(((e_re, e_im, c_e, s_e), (o_re, o_im, c_o, s_o))):
            for value in turned(re, im, c, s):
                parts.append(product(pieces(value), [high_ref[b, t], low_s[b, t]]))
        for half in range(2):
            acc[half] += parts[half] + parts[half + 2]
        return carry

    lax.fori_loop(0, BLOCKS, step, 0, unroll=8)
    lane = lax.broadcasted_iota(jnp.int32, (8, 128), 1)
    group = (lane >> 2) & 3
    plane = z[0:8]
    for n in range(1, 4):
        plane = jnp.where(group == n, z[8 * n : 8 * n + 8], plane)
    v = 256 * j + 128 * (d >> 4) + 16 * (lane >> 4) + (d & 15)
    c, s = cos_sin(chirp_turns(plane, jnp.where(v < NX // 2, v, v - NX)))
    s = -s
    for half in range(2):
        cols = slice(128 * half, 128 * half + 128)
        for part in range(2):
            for n, v in enumerate(swapped([acc[part, 8 * i : 8 * i + 8, cols] for i in range(32)], 4)):
                bands[part, 32 * half + n] = v
    for n in range(64):
        re, im = bands[0, n], bands[1, n]
        bands[0, n] = re * c - im * s
        bands[1, n] = re * s + im * c
    slot = lane & 3
    for n in range(64):
        zero = jnp.zeros((8, 128), F32)
        above = [bands[part, n - 1] if n > 0 else zero for part in range(2)]
        below = [bands[part, n + 1] if n < 63 else zero for part in range(2)]
        rim = jnp.where(
            slot < 2,
            jnp.where(slot == 0, pltpu.roll(above[0], 125, 1), pltpu.roll(below[0], 1, 1)),
            jnp.where(slot == 2, pltpu.roll(above[1], 127, 1), pltpu.roll(below[1], 3, 1)),
        )
        item = 2 * ((n & 3) * 16 + (n >> 2))
        first, second = packed(bands[0, n], bands[1, n], rim)
        out_ref[pl.ds(item, 8, stride=128), :] = first
        out_ref[pl.ds(item + 1, 8, stride=128), :] = second


def times_i(v):
    return -v[1], v[0]


def add(a, b):
    return a[0] + b[0], a[1] + b[1]


def sub(a, b):
    return a[0] - b[0], a[1] - b[1]


def times(a, c, s):
    return a[0] * c - a[1] * s, a[0] * s + a[1] * c


def four(a0, a1, a2, a3):
    p, q, m, n = add(a0, a2), add(a1, a3), sub(a0, a2), times_i(sub(a1, a3))
    return add(p, q), add(m, n), sub(p, q), sub(m, n)


def sixteen(a):
    inner = [four(a[r], a[r + 4], a[r + 8], a[r + 12]) for r in range(4)]
    out = [None] * 16
    for k in range(4):
        row = []
        for r in range(4):
            t = r * k
            v = inner[r][k]
            row.append(v if t == 0 else times(v, math.cos(math.pi * t / 8), math.sin(math.pi * t / 8)))
        for m, v in enumerate(four(*row)):
            out[k + 4 * m] = v
    return out


def row_kernel(in_ref, par_ref, row_ref, twist_ref, out_ref, x_s, a_s, b_s, power, re_s, im_s):
    d, _, _ = places()
    g = d >> 2
    for quad in range(4):
        rows = [[], [], []]
        for n in range(4):
            for half in range(2):
                start = 32 * (4 * quad + n + 16 * half)
                words = [in_ref[pl.ds(start + m, 16, stride=2), :] for m in range(2)]
                for piece, value in enumerate(unpacked(*words)):
                    rows[piece].append(value)
        for piece in range(3):
            turned = jnp.concatenate(rows[piece], axis=0).T
            for a in range(2):
                parts = swapped([turned[64 * a + 16 * n : 64 * a + 16 * n + 16] for n in range(4)], 32)
                for n, part in enumerate(parts):
                    x_s[4 * quad + n, 16 * piece : 16 * piece + 16, 128 * a : 128 * a + 128] = part
    left = pieces(x_s[...].reshape(768, HALF))
    a_s[...] = product(left, [row_ref[0, n] for n in range(PIECES)]).reshape(16, 48, HALF)
    b_s[...] = product(left, [row_ref[1, n] for n in range(PIECES)]).reshape(16, 48, HALF)
    for half in range(2):
        lanes = slice(128 * half, 128 * half + 128)
        for band in range(4):
            here = slice(8 * band, 8 * band + 8)
            values = []
            for k in range(16):
                if band < 2:
                    low = slice(16 + 8 * band, 24 + 8 * band)
                    re = a_s[k, here, lanes] - b_s[k, low, lanes]
                    im = b_s[k, here, lanes] + a_s[k, low, lanes]
                else:
                    rim = slice(16 + 8 * band, 24 + 8 * band)
                    a, b = a_s[k, rim, lanes], b_s[k, rim, lanes]
                    re = a - pltpu.roll(b, 6, 0)
                    im = b + pltpu.roll(a, 6, 0)
                values.append(times((re, im), twist_ref[0, k : k + 1, lanes], twist_ref[1, k : k + 1, lanes]))
            for k, (re, im) in enumerate(sixteen(values)):
                spot = slice(256 * k + 128 * half, 256 * k + 128 * half + 128)
                if band < 2:
                    re_s[here, spot] = re
                    im_s[here, spot] = im
                power[here, spot] = re * re + im * im
    here = power[0:16]
    rim = power[16:32]
    row = lax.broadcasted_iota(jnp.int32, (16, NX), 0)
    lane = lax.broadcasted_iota(jnp.int32, (16, NX), 1)
    up = jnp.where((row & 3) == 0, rim, pltpu.roll(here, 1, 0))
    down = jnp.where((row & 3) == 3, pltpu.roll(rim, 2, 0), pltpu.roll(here, 15, 0))

    def moved(v, offset):
        if offset > 0:
            return jnp.where(lane < NX - offset, pltpu.roll(v, NX - offset, 1), 0.0)
        return jnp.where(lane >= -offset, pltpu.roll(v, -offset, 1), 0.0)

    row_small = lax.broadcasted_iota(jnp.int32, (16, 128), 0) >> 2

    def of_rows(which):
        value = jnp.zeros((16, 128), F32)
        for n in range(4):
            value = jnp.where(row_small == n, par_ref[which, pl.ds(8 * n + g, 1), :], value)
        return value[:, 0:1]

    depth, radius, gain = of_rows(0) * (1.0 / DEPTHS), of_rows(1), of_rows(2)
    vertical = up + 2.0 * here + down
    step = down - up
    across = moved(vertical, 1) - moved(vertical, -1)
    downward = moved(step, -1) + 2.0 * step + moved(step, 1)
    energy = across * across + downward * downward
    total = energy
    for offset in range(1, MAXWIDTH + 1):
        inside = (offset <= radius).astype(F32)
        total = total + inside * (moved(energy, -offset) + moved(energy, offset))
    smoothed = total / (2.0 * radius + 1.0)
    scores = gain * jnp.log(1.0 + smoothed)
    peak = jnp.maximum(scores[0:8], scores[8:16])
    peak = jnp.maximum(peak, pltpu.roll(peak, 4, 0))
    first, second = jnp.exp(scores[0:8] - peak), jnp.exp(scores[8:16] - peak)

    def joined(v):
        return (v + pltpu.roll(v, 4, 0))[0:4]

    records = (
        peak[0:4],
        joined(first + second),
        joined(first * depth[0:8] + second * depth[8:16]),
        joined(first * re_s[0:8] + second * re_s[8:16]),
        joined(first * im_s[0:8] + second * im_s[8:16]),
    )
    for n, record in enumerate(records):
        for target in range(32):
            out_ref[target, n] = record[:, 128 * target : 128 * target + 128]


def merge_kernel(in_ref, depth_ref, focus_ref):
    for q in range(4):
        spots = [4 * g + q for g in range(8)]
        peak = in_ref[spots[0], 0]
        for n in spots[1:]:
            peak = jnp.maximum(peak, in_ref[n, 0])
        weights = [jnp.exp(in_ref[n, 0] - peak) for n in spots]
        sums = [sum(w * in_ref[n, k] for w, n in zip(weights, spots)) for k in range(1, 5)]
        rows = slice(4 * q, 4 * q + 4)
        depth_ref[rows] = sums[1] / sums[0]
        focus_ref[0, rows] = sums[2] / sums[0]
        focus_ref[1, rows] = sums[3] / sums[0]


def params(mib):
    return pltpu.CompilerParams(vmem_limit_bytes=mib * 1024 * 1024)


def whole(shape):
    return pl.BlockSpec(shape, lambda *_: (0,) * len(shape))


def cost(flops, size):
    return pl.CostEstimate(flops=flops, bytes_accessed=size, transcendentals=0)


def shards(spectrum, plane_index, kernel_width, focus_gain):
    smem = pl.BlockSpec(memory_space=pltpu.SMEM)
    picked = pl.pallas_call(
        pick_kernel,
        in_specs=[smem, smem, smem, pl.BlockSpec(memory_space=pl.ANY)],
        out_specs=whole((32, 24, 128)),
        out_shape=jax.ShapeDtypeStruct((32, 24, 128), BF16),
        scratch_shapes=[pltpu.VMEM((2, 128, 256), BF16), pltpu.SemaphoreType.DMA(())],
        compiler_params=params(58),
        cost_estimate=cost(50_000_000, 300_000),
        name="pick",
    )(plane_index, kernel_width, focus_gain, spectrum)
    groups = [[16 * d + (d + j) % 16 for d in range(32)] for j in range(16)]
    columns = lax.all_to_all(
        picked, ALL, split_axis=0, concat_axis=0, tiled=True, axis_index_groups=groups
    )

    high, low, row_table, twist = pl.pallas_call(
        table_kernel,
        grid=(BLOCKS,),
        in_specs=[],
        out_specs=[
            pl.BlockSpec((1, 2, HALF, HALF), lambda b: (b, 0, 0, 0)),
            pl.BlockSpec((1, 2, HALF, HALF), lambda b: (b, 0, 0, 0)),
            whole((2, PIECES, HALF, HALF)),
            whole((2, 16, HALF)),
        ],
        out_shape=[
            jax.ShapeDtypeStruct((BLOCKS, 2, HALF, HALF), BF16),
            jax.ShapeDtypeStruct((BLOCKS, 2, HALF, HALF), BF16),
            jax.ShapeDtypeStruct((2, PIECES, HALF, HALF), BF16),
            jax.ShapeDtypeStruct((2, 16, HALF), F32),
        ],
        scratch_shapes=[pltpu.VMEM((HALF, HALF), F32), pltpu.VMEM((HALF, HALF), F32)],
        compiler_params=params(16),
        cost_estimate=cost(30_000_000, 5_000_000),
        name="tables",
    )()

    messages, planes = pl.pallas_call(
        column_kernel,
        in_specs=[
            whole((32, 24, 128)),
            whole((BLOCKS, 2, HALF, HALF)),
            pl.BlockSpec(memory_space=pl.ANY),
        ],
        out_specs=[whole((1024, 128)), whole((3, 32, 128))],
        out_shape=[
            jax.ShapeDtypeStruct((1024, 128), jnp.int32),
            jax.ShapeDtypeStruct((3, 32, 128), F32),
        ],
        scratch_shapes=[
            pltpu.VMEM((2, HALF, HALF), F32),
            pltpu.VMEM((256, 128), F32),
            pltpu.VMEM((2, 64, 8, 128), F32),
            pltpu.VMEM((BLOCKS, 2, HALF, HALF), BF16),
            pltpu.SemaphoreType.DMA((BLOCKS,)),
        ],
        compiler_params=params(50),
        cost_estimate=cost(6_500_000_000, 8_000_000),
        name="columns",
    )(columns, high, low)
    arrived = lax.all_to_all(
        messages.reshape(512, 1, 256), ALL, split_axis=0, concat_axis=0, tiled=True
    )

    records = pl.pallas_call(
        row_kernel,
        in_specs=[
            whole((1024, 128)),
            whole((3, 32, 128)),
            whole((2, PIECES, HALF, HALF)),
            whole((2, 16, HALF)),
        ],
        out_specs=whole((32, 5, 4, 128)),
        out_shape=jax.ShapeDtypeStruct((32, 5, 4, 128), F32),
        scratch_shapes=[
            pltpu.VMEM((16, 48, HALF), F32),
            pltpu.VMEM((16, 48, HALF), F32),
            pltpu.VMEM((16, 48, HALF), F32),
            pltpu.VMEM((32, NX), F32),
            pltpu.VMEM((16, NX), F32),
            pltpu.VMEM((16, NX), F32),
        ],
        compiler_params=params(24),
        cost_estimate=cost(1_000_000_000, 2_200_000),
        name="rows",
    )(arrived.reshape(1024, 128), planes, row_table, twist)
    merged = lax.all_to_all(records, "depth", split_axis=0, concat_axis=0, tiled=True)

    depth_map, focused = pl.pallas_call(
        merge_kernel,
        in_specs=[whole((32, 5, 4, 128))],
        out_specs=[whole((16, 128)), whole((2, 16, 128))],
        out_shape=[
            jax.ShapeDtypeStruct((16, 128), F32),
            jax.ShapeDtypeStruct((2, 16, 128), F32),
        ],
        compiler_params=params(4),
        cost_estimate=cost(1_000_000, 500_000),
        name="merge",
    )(merged)
    return depth_map, focused


def solution(mesh):
    return jax.shard_map(
        shards,
        mesh=mesh,
        in_specs=(P(None, "rows", None), P("depth"), P("depth"), P("depth")),
        out_specs=(P("rows", "depth"), P(None, "rows", "depth")),
        check_vma=False,
    )
```
